32 devices in a mesh: py: 4 (over z), pz: 8 (over y, x, core).
Axes of the slice: x: 2, y: 2, z: 4, core: 2. Of those that a mesh axis runs over, the one named last changes fastest.
Arguments:
- start: float32 [32, 64, 512], P('py', 'pz'), may hold values from -36 to 36
- coef_x: float32 [32, 64, 512], P('py', 'pz'), may hold values from 0.5 to 2
- coef_y: float32 [32, 64, 512], P('py', 'pz'), may hold values from 0.5 to 2
- coef_z: float32 [32, 64, 512], P('py', 'pz'), may hold values from 0.5 to 2
- shifts: float32 [8], replicated, may hold values from 0 to 14
Outputs:
- orthonormal: float32 [9, 32, 64, 512], P(None, 'py', 'pz')
- triangle: float32 [9, 9], replicated
The draws below stay inside these ranges and needn't reach their ends.
All inputs are finite; a program needn't handle non-finite values.
Results may differ from the reference program's by a relative error of at most 0.0003.
Values sent between devices are 32-bit elements; how exact they have to be, the bound alone decides.
A program may use at most 128 MiB of HBM per device.

```python
import math
import jax
import jax.numpy as jnp
from jax import lax

NX = 512
S = 8
BASIS = 9
NY = 32
NZ = 64


def draw_start(key, part):
    first, second = jax.random.split(jax.random.fold_in(key, 11))
    shape = (NY, NZ, NX)
    spread = jnp.exp(jax.random.uniform(first, shape, jnp.float32, 0.0, math.log(10.0)))
    trend_y = 1.0 + 2.0 * jnp.arange(NY, dtype=jnp.float32) / max(NY - 1, 1)
    trend_z = 1.0 + 2.0 * jnp.arange(NZ, dtype=jnp.float32) / max(NZ - 1, 1)
    trend = trend_y[:, None, None] * trend_z[None, :, None]
    base = jnp.clip(jax.random.normal(second, shape, jnp.float32), -4.0, 4.0)
    return (base * spread * trend * 0.1).astype(jnp.float32)


def draw_shifts(key, part):
    order = jnp.arange(S, dtype=jnp.int32)
    flipped = (order & 1) << 2 | order & 2 | order >> 2 & 1
    nodes = 7.0 + 6.0 * jnp.cos(math.pi * (2.0 * flipped.astype(jnp.float32) + 1.0) / (2.0 * S))
    jitter = jax.random.uniform(jax.random.fold_in(key, 23), (S,), jnp.float32, -1.0, 1.0)
    return (nodes + jitter).astype(jnp.float32)


def levels(own_key, extent, pieces, smallest, largest):
    level, own = 1.0, jax.random.fold_in(own_key, 6)
    for axis_at, shards_of in pieces:
        draws = jnp.exp(jax.random.uniform(jax.random.fold_in(own, axis_at), (shards_of,), jnp.float32, smallest / len(pieces), largest / len(pieces)))
        level = level * jnp.repeat(draws, extent[axis_at] // shards_of).reshape([-1 if axis == axis_at else 1 for axis in range(len(extent))])
    return level


def setup_inputs(seed: int = 0) -> dict:
    splits = jax.random.split(jax.random.key(seed), 6)
    return {
        "start": draw_start(jax.random.fold_in(splits[5], 71), 0),
        "coef_x": jnp.clip(jnp.exp(math.log(2.0) - 1.3862944 * jax.random.uniform(splits[1], (NY, NZ, NX), jnp.float32) ** levels(splits[1], (NY, NZ, NX), ((0, 4), (1, 8)), -0.2, 0.2)), 0.5, 2.0),
        "coef_y": jnp.clip(jnp.exp(math.log(2.0) - 1.3862944 * jax.random.uniform(splits[2], (NY, NZ, NX), jnp.float32) ** levels(splits[2], (NY, NZ, NX), ((0, 4), (1, 8)), -0.2, 0.2)), 0.5, 2.0),
        "coef_z": jnp.clip(jnp.exp(math.log(2.0) - 1.3862944 * jax.random.uniform(splits[3], (NY, NZ, NX), jnp.float32) ** levels(splits[3], (NY, NZ, NX), ((0, 4), (1, 8)), -0.2, 0.2)), 0.5, 2.0),
        "shifts": draw_shifts(jax.random.fold_in(splits[5], 71), 0),
    }


def below_cells(array, dim):
    edge = jnp.zeros_like(lax.slice_in_dim(array, 0, 1, axis=dim))
    return jnp.concatenate([edge, lax.slice_in_dim(array, 0, array.shape[dim] - 1, axis=dim)], axis=dim)

def above_cells(array, dim):
    edge = jnp.zeros_like(lax.slice_in_dim(array, 0, 1, axis=dim))
    return jnp.concatenate([lax.slice_in_dim(array, 1, array.shape[dim], axis=dim), edge], axis=dim)

def operate(field, coef_x, coef_y, coef_z):
    result = jnp.zeros_like(field)
    for dim, coef in ((2, coef_x), (0, coef_y), (1, coef_z)):
        result = result + coef * (field - above_cells(field, dim))
        result = result + below_cells(coef, dim) * (field - below_cells(field, dim))
    return result

def forward(factor, vectors):
    count = factor.shape[0]
    solved = []
    for row in range(count):
        partial_sum = vectors[row]
        for inner in range(row):
            partial_sum = partial_sum - factor[inner, row] * solved[inner]
        solved.append(partial_sum / factor[row, row])
    return jnp.stack(solved)

def reference(start, coef_x, coef_y, coef_z, shifts):
    vectors = [start]
    current = start
    for level in range(S):
        image = operate(current, coef_x, coef_y, coef_z)
        current = (image - shifts[level] * current) * 0.125
        vectors.append(current)
    basis = jnp.stack(vectors)
    flat = basis.reshape(BASIS, NY, NZ * NX)

    def block_factor(index_y):
        tall = lax.dynamic_index_in_dim(flat, index_y, axis=1, keepdims=False).T
        return jnp.linalg.qr(tall, mode='r')
    blocks = lax.map(block_factor, jnp.arange(NY, dtype=jnp.int32))
    upper = jnp.linalg.qr(blocks.reshape(NY * BASIS, BASIS), mode='r')
    signs = jnp.where(jnp.diagonal(upper) >= 0, 1.0, -1.0).astype(upper.dtype)
    triangle = upper * signs[:, None] / math.sqrt(NX * NY * NZ)
    orthonormal = forward(triangle, basis.reshape(BASIS, -1)).reshape(basis.shape)
    return (orthonormal, triangle)
```

```python
import functools
import math

import jax
import jax.numpy as jnp
from jax import lax
from jax.experimental import pallas as pl
from jax.experimental.pallas import tpu as pltpu
from jax.sharding import PartitionSpec as P

step_scale = 0.125
MESH = pl.DeviceIdType.MESH
LANES = 128
SUBLANES = 8
WAYS = ((1, 0), (-1, 0), (0, 1), (0, -1), (1, 1), (1, -1), (-1, 1), (-1, -1))


def two_sum(a, b):
    total = a + b
    virtual = total - a
    return total, (a - (total - virtual)) + (b - virtual)


def split(a):
    scaled = a * 4097.0
    high = scaled - (scaled - a)
    return high, a - high


def two_product(a, b):
    product = a * b
    a_high, a_low = split(a)
    b_high, b_low = split(b)
    error = ((a_high * b_high - product) + a_high * b_low + a_low * b_high) + a_low * b_low
    return product, error


def pair_add(a, b):
    total, error = two_sum(a[0], b[0])
    return total, error + (a[1] + b[1])


def renormal(a):
    total = a[0] + a[1]
    return total, a[1] - (total - a[0])


def tree(parts):
    while len(parts) > 1:
        rest = parts[len(parts) // 2 * 2 :]
        parts = [pair_add(parts[i], parts[i + 1]) for i in range(0, len(parts) - 1, 2)] + rest
    return parts[0]


def sum_pairs(parts):
    while len(parts) > 1:
        rest = parts[len(parts) // 2 * 2 :]
        added = []
        for i in range(0, len(parts) - 1, 2):
            total, error = two_sum(parts[i][0], parts[i + 1][0])
            added.append((total, error + (parts[i][1] + parts[i + 1][1])))
        parts = added + rest
    return parts[0]


def sum_rows(tiles):
    zero = jnp.zeros_like(tiles[0])
    total = sum_pairs([(tile, zero) for tile in tiles])
    shift = SUBLANES // 2
    while shift:
        total = pair_add(total, tuple(pltpu.roll(piece, shift, 0) for piece in total))
        shift //= 2
    return total


def fold(total):
    lead, minor = total
    return renormal((lead, minor + pltpu.roll(lead + minor, LANES // 2, 1)))


def wrap(high, low):
    lane = lax.broadcasted_iota(jnp.int32, high.shape, 1)
    return jnp.where(lane < LANES // 2, high, pltpu.roll(low, LANES // 2, 1))


def plan(depth):
    groups = [1]
    while sum(groups) < depth:
        groups.append(min(4 if len(groups) > 1 else 3, depth - sum(groups)))
    return tuple(groups)


def stages_of(count_y, count_z):
    if count_y * count_z <= 64:
        return (("py", "pz"),)
    return (("pz",), ("py",))


def first_pair(column):
    return column * (column + 1) // 2


def kernel(
    groups,
    count_y,
    count_z,
    root_cells,
    start_hbm,
    x_hbm,
    y_hbm,
    z_hbm,
    shifts,
    basis,
    triangle,
    ghost,
    work,
    coef,
    mask,
    partial,
    row_source,
    *rest,
):
    stages = stages_of(count_y, count_z)
    row_buffers = rest[: len(stages)]
    load_sem, send_sem, recv_sem, coef_send, coef_recv, row_send, row_recv = rest[len(stages) :]
    depth = shifts.shape[0]
    count = depth + 1
    _, rows_y, rows_z, length = basis.shape
    span_y, span_z = ghost.shape[1:3]
    padded = triangle.shape[0]
    sizes = {"py": count_y, "pz": count_z}
    me = {"py": lax.axis_index("py"), "pz": lax.axis_index("pz")}
    me_y, me_z = me["py"], me["pz"]
    most = max(groups)

    has = []
    comes = []
    target = []
    for dy, dz in WAYS:
        ahead, behind = [], []
        for step, at, size in ((dy, me_y, count_y), (dz, me_z, count_z)):
            if step:
                up, down = at < size - 1, at > 0
                ahead.append(up if step > 0 else down)
                behind.append(down if step > 0 else up)
        has.append(functools.reduce(jnp.logical_and, ahead))
        comes.append(functools.reduce(jnp.logical_and, behind))
        target.append({"py": me_y + dy, "pz": me_z + dz})

    barrier = pltpu.get_barrier_semaphore()
    if len(stages) == 1:
        expected = count_y * count_z - 1

        def greet(away, carry):
            other = lax.rem(me_y * count_z + me_z + away, count_y * count_z)
            pl.semaphore_signal(
                barrier,
                inc=1,
                device_id={"py": lax.div(other, count_z), "pz": lax.rem(other, count_z)},
                device_id_type=MESH,
            )
            return carry

        lax.fori_loop(1, count_y * count_z, greet, 0)
    else:
        expected = count_y + count_z - 2
        for axis, size in sizes.items():
            def greet(away, carry):
                pl.semaphore_signal(
                    barrier, inc=1, device_id={axis: lax.rem(me[axis] + away, size)}, device_id_type=MESH
                )
                return carry

            lax.fori_loop(1, size, greet, 0)
        for way in range(4, 8):
            pl.when(has[way])(
                lambda way=way: pl.semaphore_signal(
                    barrier, inc=1, device_id=target[way], device_id_type=MESH
                )
            )
            expected = expected + jnp.where(comes[way], 1, 0)

    own = (pl.ds(0, rows_y), pl.ds(0, rows_z))
    loads = [
        pltpu.make_async_copy(source, place, load_sem.at[i])
        for i, (source, place) in enumerate(
            (
                (start_hbm, basis.at[0]),
                (z_hbm, coef.at[2, own[0], own[1]]),
                (y_hbm, coef.at[1, own[0], own[1]]),
                (x_hbm, coef.at[0, own[0], own[1]]),
            )
        )
    ]
    for load in loads:
        load.start()

    def ends(step, rows, span, first, last):
        if step > 0:
            return pl.ds(rows - last, last - first), pl.ds(span - last, last - first)
        if step < 0:
            return pl.ds(first, last - first), pl.ds(rows + first, last - first)
        return pl.ds(0, rows), pl.ds(0, rows)

    def copy(source, place, way, y_band, z_band, sends, recvs, index):
        dy, dz = WAYS[way]
        from_y, to_y = ends(dy, rows_y, span_y, *y_band)
        from_z, to_z = ends(dz, rows_z, span_z, *z_band)
        return way, pltpu.make_async_remote_copy(
            src_ref=source.at[from_y, from_z],
            dst_ref=place.at[to_y, to_z],
            send_sem=sends.at[index],
            recv_sem=recvs.at[index],
            device_id=target[way],
            device_id_type=MESH,
        )

    def start_all(copies):
        for way, each in copies:
            pl.when(has[way])(lambda each=each: each.start())

    def arrive_all(copies):
        for way, each in copies:
            pl.when(comes[way])(lambda each=each: each.wait_recv())

    def leave_all(copies):
        for way, each in copies:
            pl.when(has[way])(lambda each=each: each.wait_send())

    def field_copies(group):
        slot, reach = sum(groups[:group]), groups[group]
        ways = range(8) if reach > 1 else range(4)
        bands = lambda way: (0, reach) if way < 4 else (0, reach - 1)
        return [
            copy(
                basis.at[slot], ghost.at[group], way, bands(way), bands(way), send_sem, recv_sem, group * 8 + way
            )
            for way in ways
        ]

    def coef_copies():
        early, late = [], []
        index = 0
        for which in (1, 2, 0):
            for way, (dy, dz) in enumerate(WAYS):
                corner = way >= 4
                below = (which == 1 and dy > 0) or (which == 2 and dz > 0)
                y_last = z_last = most - (2 if corner else 1) + (1 if below else 0)
                first = 0
                if below and not corner:
                    early.append(
                        copy(coef.at[which], coef.at[which], way, (0, 1), (0, 1), coef_send, coef_recv, index)
                    )
                    index += 1
                    first = 1
                if y_last > first and z_last > first:
                    late.append(
                        copy(
                            coef.at[which],
                            coef.at[which],
                            way,
                            (first, y_last),
                            (first, z_last),
                            coef_send,
                            coef_recv,
                            index,
                        )
                    )
                    index += 1
        return early, late

    fields = [field_copies(group) for group in range(len(groups))]
    early, late = coef_copies()

    loads[0].wait()
    loads[1].wait()
    loads[2].wait()
    pl.semaphore_wait(barrier, expected)
    start_all(fields[0])
    start_all(early)
    loads[3].wait()
    start_all(late)

    def clear(block_y, block_z):
        for buffer, pieces in ((ghost, len(groups)), (coef, 3)):
            for piece in range(pieces):
                shape = (block_y[1], block_z[1], length)
                buffer[piece, pl.ds(*block_y), pl.ds(*block_z), :] = jnp.zeros(shape, jnp.float32)

    reach_y, reach_z = span_y - rows_y, span_z - rows_z
    half_y, half_z = reach_y // 2, reach_z // 2
    pl.when(me_y == 0)(lambda: clear((rows_y + half_y, half_y), (0, span_z)))
    pl.when(me_y == count_y - 1)(lambda: clear((rows_y, half_y), (0, span_z)))
    pl.when(me_z == 0)(lambda: clear((0, span_y), (rows_z + half_z, half_z)))
    pl.when(me_z == count_z - 1)(lambda: clear((0, span_y), (rows_z, half_z)))

    lane = lax.broadcasted_iota(jnp.int32, (rows_z, length), 1)
    sub = lax.broadcasted_iota(jnp.int32, (rows_z, length), 0)
    inside_z = jnp.where(
        sub < half_z,
        jnp.where(me_z < count_z - 1, step_scale, 0.0),
        jnp.where(me_z > 0, step_scale, 0.0),
    )
    inside_below = jnp.where(me_y > 0, 1.0, 0.0)
    inside_above = jnp.where(me_y < count_y - 1, 1.0, 0.0)
    mask[0] = inside_z
    mask[1] = inside_z * inside_below
    mask[2] = inside_z * inside_above

    main, outer = pl.ds(0, rows_z), pl.ds(rows_z, span_z - rows_z)

    def level(group, step):
        slot = sum(groups[:group]) + step
        left = groups[group] - step - 1
        shift = shifts[slot]
        source = ghost.at[group] if step == 0 else work.at[(step - 1) % 2]
        place = work.at[step % 2]
        values, fluxes = {}, {}

        def value(y, tile):
            if (y, tile) not in values:
                if tile == 0 and 0 <= y < rows_y:
                    values[y, tile] = basis[slot, y]
                else:
                    values[y, tile] = source[y % span_y, outer if tile else main, :]
            return values[y, tile]

        def flux_y(y, tile):
            if (y, tile) not in fluxes:
                fluxes[y, tile] = coef[1, y % span_y, outer if tile else main, :] * (
                    value(y, tile) - value(y + 1, tile)
                )
            return fluxes[y, tile]

        for y in range(-left, rows_y + left):
            off = max(0, -y, y - rows_y + 1)
            tiles = (0, 1) if left - off >= 1 else (0,)
            if len(tiles) == 2:
                rows = [value(y, tile) for tile in (0, 1)]
                turned = [pltpu.roll(row, rows_z - 1, 0) for row in rows]
                flux_z = []
                for tile in (0, 1):
                    up = jnp.where(sub == rows_z - 1, turned[1 - tile], turned[tile])
                    flux_z.append(coef[2, y % span_y, outer if tile else main, :] * (rows[tile] - up))
                turned = [pltpu.roll(flux, 1, 0) for flux in flux_z]
            else:
                rows = [value(y, 0)]
                up = jnp.where(
                    sub == rows_z - 1,
                    source[y % span_y, pl.ds(rows_z, 1), :],
                    pltpu.roll(rows[0], rows_z - 1, 0),
                )
                flux_z = [coef[2, y % span_y, main, :] * (rows[0] - up)]
                below = coef[2, y % span_y, pl.ds(span_z - 1, 1), :] * (
                    source[y % span_y, pl.ds(span_z - 1, 1), :] - rows[0][0:1, :]
                )
                turned = [pltpu.roll(flux_z[0], 1, 0), below]
            for tile in tiles:
                row = rows[tile]
                here = outer if tile else main
                ahead = jnp.where(lane == length - 1, 0.0, pltpu.roll(row, length - 1, 1))
                flux_x = coef[0, y % span_y, here, :] * (row - ahead)
                image = flux_x - jnp.where(lane == 0, 0.0, pltpu.roll(flux_x, 1, 1))
                image = image + flux_y(y, tile)
                image = image - flux_y(y - 1, tile)
                image = image + flux_z[tile]
                image = image - jnp.where(sub == 0, turned[1 - tile], turned[tile])
                fresh = image - shift * row
                zone = 1 if y < 0 else 2 if y >= rows_y else 0
                if tile:
                    fresh = fresh * mask[zone]
                else:
                    fresh = fresh * step_scale
                    if zone:
                        fresh = fresh * (inside_below if zone == 1 else inside_above)
                if tile == 0 and zone == 0:
                    basis[slot + 1, y] = fresh
                else:
                    place[y % span_y, here, :] = fresh

    def gram(columns):
        pairs = [(i, j) for j in columns for i in range(j + 1)]

        def plane(y, totals):
            totals = list(totals)
            for x in range(0, length, LANES):
                pieces = [basis[i, y, :, x : x + LANES] for i in range(max(columns) + 1)]
                for p, (i, j) in enumerate(pairs):
                    totals[p] = totals[p] + pieces[i] * pieces[j]
            return tuple(totals)

        zero = jnp.zeros((SUBLANES, LANES), jnp.float32)
        totals = lax.fori_loop(0, rows_y, plane, (zero,) * len(pairs))
        for (i, j), total in zip(pairs, totals):
            partial[pl.ds((first_pair(j) + i) * SUBLANES, SUBLANES), :] = total

    pairs = first_pair(count)
    many = partial.shape[0] // SUBLANES
    for at in range(pairs, many):
        partial[pl.ds(at * SUBLANES, SUBLANES), :] = jnp.zeros((SUBLANES, LANES), jnp.float32)

    for group, applications in enumerate(groups):
        if group == 1:
            arrive_all(late)
        if group:
            start_all(fields[group])
            gram(range(0 if group == 1 else sum(groups[: group - 1]) + 1, sum(groups[:group]) + 1))
        arrive_all(fields[group])
        if group == 0:
            arrive_all(early)
        for step in range(applications):
            level(group, step)
    gram(range(sum(groups[:-1]) + 1, count))

    high, low = sum_pairs(
        [
            (partial[pl.ds(s, many, stride=SUBLANES), :], jnp.zeros((many, LANES), jnp.float32))
            for s in range(SUBLANES)
        ]
    )
    fill = jnp.zeros((LANES // 2 - many, LANES), jnp.float32)
    turned = jnp.concatenate([high, fill, low, fill], axis=0).T
    total = fold(sum_rows([turned[y : y + SUBLANES] for y in range(0, LANES, SUBLANES)]))
    for stage, axes in enumerate(stages):
        buffer = row_buffers[stage]
        size = math.prod(sizes[axis] for axis in axes)
        index = functools.reduce(lambda at, axis: at * sizes[axis] + me[axis], axes, 0)
        row_source[stage] = wrap(*total)
        if buffer.shape[0] > size:
            buffer[pl.ds(size, buffer.shape[0] - size), :] = jnp.zeros(
                (buffer.shape[0] - size, LANES), jnp.float32
            )

        def send(away, carry):
            other = lax.rem(index + away, size)
            device = {}
            for axis in reversed(axes):
                device[axis] = lax.rem(other, sizes[axis])
                other = lax.div(other, sizes[axis])
            pltpu.make_async_remote_copy(
                src_ref=row_source.at[stage, pl.ds(0, 1)],
                dst_ref=buffer.at[pl.ds(index, 1)],
                send_sem=row_send.at[stage],
                recv_sem=row_recv.at[stage],
                device_id=device,
                device_id_type=MESH,
            ).start()
            return carry

        lax.fori_loop(1, size, send, 0)
        buffer[pl.ds(index, 1), :] = row_source[stage, pl.ds(0, 1), :]
        if stage == 0:
            for copies in (*fields, early, late):
                leave_all(copies)
        others = buffer.at[pl.ds(0, size - 1)]
        pltpu.make_async_copy(others, others, row_recv.at[stage]).wait()
        pltpu.make_async_copy(others, others, row_send.at[stage]).wait()
        rows = [buffer[pl.ds(y, SUBLANES), :] for y in range(0, buffer.shape[0], SUBLANES)]
        total = fold(sum_rows(rows))

    square_sub = lax.broadcasted_iota(jnp.int32, (padded, LANES), 0)
    square_lane = lax.broadcasted_iota(jnp.int32, (padded, LANES), 1)
    zero = jnp.zeros((padded, LANES), jnp.float32)
    lower = []
    for piece in total:
        piece = jnp.concatenate([piece] * (padded // SUBLANES), axis=0)
        square = zero
        for column in range(count):
            at = first_pair(column)
            moved = pltpu.roll(piece, LANES - at, 1) if at else piece
            square = jnp.where(jnp.logical_and(square_sub == column, square_lane <= column), moved, square)
        lower.append(square)
    fill = jnp.zeros((LANES - 2 * padded, LANES), jnp.float32)
    turned = jnp.concatenate([*lower, fill], axis=0).T[:padded]
    g_high = jnp.where(square_lane < square_sub, lower[0], turned)
    g_low = jnp.where(square_lane < square_sub, lower[1], pltpu.roll(turned, LANES - padded, 1))

    tri = zero
    row_lane = lax.broadcasted_iota(jnp.int32, (1, LANES), 1)
    for k in range(count):
        row_high, row_low = g_high[k : k + 1, :], g_low[k : k + 1, :]
        d_high = jnp.broadcast_to(row_high[:, k : k + 1], (1, LANES))
        d_low = jnp.broadcast_to(row_low[:, k : k + 1], (1, LANES))
        within = jnp.logical_and(row_lane >= k, row_lane < count)
        factor = jnp.where(within, row_high / jnp.sqrt(d_high) / root_cells, 0.0)
        tri = jnp.where(square_sub == k, factor, tri)
        if k == count - 1:
            break
        inverse = 1.0 / d_high
        lead = row_high * inverse
        product, error = two_product(lead, d_high)
        minor = (((row_high - product) - error) + (row_low - lead * d_low)) * inverse
        col_high = jnp.broadcast_to(g_high[:, k : k + 1], (padded, LANES))
        col_low = jnp.broadcast_to(g_low[:, k : k + 1], (padded, LANES))
        lead = jnp.broadcast_to(lead, (padded, LANES))
        minor = jnp.broadcast_to(minor, (padded, LANES))
        product, error = two_product(col_high, lead)
        error = error + (col_high * minor + col_low * lead)
        total, rest_of = two_sum(g_high, -product)
        g_high, g_low = renormal((total, rest_of + (g_low - error)))
    triangle[...] = tri


def substitute(basis, factor, out, triangle, splat):
    count, rows_y, rows_z, length = out.shape
    first = pl.program_id(0) * rows_y

    @pl.when(pl.program_id(0) == 0)
    def _():
        tri = factor[...]
        triangle[...] = tri[:count, :count]
        for k in range(count):
            for i in range(k, count):
                value = jnp.broadcast_to(tri[k : k + 1, i : i + 1], (SUBLANES, LANES))
                splat[k * count + i] = 1.0 / value if i == k else value

    def plane(y, carry):
        for x in range(0, length, LANES):
            solved = []
            for i in range(count):
                value = basis[i, first + y, :, x : x + LANES]
                for k in range(i):
                    value = value - splat[k * count + i] * solved[k]
                value = value * splat[i * count + i]
                out[i, y, :, x : x + LANES] = value
                solved.append(value)
        return carry

    lax.fori_loop(0, rows_y, plane, 0)


def on_device(start, coef_x, coef_y, coef_z, shifts):
    rows_y, rows_z, length = start.shape
    depth = shifts.shape[0]
    count = depth + 1
    padded = (count + SUBLANES - 1) // SUBLANES * SUBLANES
    count_y, count_z = lax.axis_size("py"), lax.axis_size("pz")
    cells = length * rows_y * rows_z * count_y * count_z
    groups = plan(depth)
    span_y, span_z = rows_y + 8, rows_z + 8
    stages = stages_of(count_y, count_z)
    sizes = {"py": count_y, "pz": count_z}
    members = [math.prod(sizes[axis] for axis in axes) for axes in stages]
    whole = pl.BlockSpec(memory_space=pltpu.VMEM)
    many = (first_pair(count) + SUBLANES - 1) // SUBLANES * SUBLANES
    pltpu_f32 = lambda *shape: pltpu.VMEM(shape, jnp.float32)
    dma = pltpu.SemaphoreType.DMA
    anywhere = pl.BlockSpec(memory_space=pl.ANY)
    basis, factor = pl.pallas_call(
        functools.partial(kernel, groups, count_y, count_z, math.sqrt(cells)),
        out_shape=(
            pltpu_f32(count, rows_y, rows_z, length),
            pltpu_f32(padded, LANES),
        ),
        in_specs=[anywhere] * 4 + [pl.BlockSpec(memory_space=pltpu.SMEM)],
        out_specs=(whole, whole),
        scratch_shapes=[
            pltpu_f32(len(groups), span_y, span_z, length),
            pltpu_f32(2, span_y, span_z, length),
            pltpu_f32(3, span_y, span_z, length),
            pltpu_f32(3, rows_z, length),
            pltpu_f32(many * SUBLANES, LANES),
            pltpu_f32(len(stages), SUBLANES, LANES),
            *[pltpu_f32((n + SUBLANES - 1) // SUBLANES * SUBLANES, LANES) for n in members],
            dma((4,)),
            dma((len(groups) * 8,)),
            dma((len(groups) * 8,)),
            dma((26,)),
            dma((26,)),
            dma((len(stages),)),
            dma((len(stages),)),
        ],
        compiler_params=pltpu.CompilerParams(collective_id=0, has_side_effects=True),
    )(start, coef_x, coef_y, coef_z, shifts)
    basis = pltpu.with_memory_space_constraint(basis, pltpu.VMEM)
    factor = pltpu.with_memory_space_constraint(factor, pltpu.VMEM)
    block = (count, max(1, rows_y // 4), rows_z, length)
    planes = pl.BlockSpec(block, lambda i: (0, i, 0, 0))
    return pl.pallas_call(
        substitute,
        grid=(rows_y // block[1],),
        out_shape=(
            jax.ShapeDtypeStruct((count, rows_y, rows_z, length), jnp.float32),
            jax.ShapeDtypeStruct((count, count), jnp.float32),
        ),
        in_specs=[whole, whole],
        out_specs=(planes, pl.BlockSpec((count, count), lambda i: (0, 0))),
        scratch_shapes=[pltpu_f32(count * count, SUBLANES, LANES)],
    )(basis, factor)


def solution(mesh):
    placed = (
        P("py", "pz", None),
        P("py", "pz", None),
        P("py", "pz", None),
        P("py", "pz", None),
        P(),
    )
    return jax.shard_map(
        on_device,
        mesh=mesh,
        in_specs=placed,
        out_specs=(P(None, "py", "pz", None), P()),
        check_vma=False,
    )
```

```python
import functools
import math

import jax
import jax.numpy as jnp
from jax import lax
from jax.experimental import pallas as pl
from jax.experimental.pallas import tpu as pltpu
from jax.sharding import PartitionSpec as P

step_scale = 0.125
MESH = pl.DeviceIdType.MESH
LANES = 128
SUBLANES = 8
WAYS = ((1, 0), (-1, 0), (0, 1), (0, -1), (1, 1), (1, -1), (-1, 1), (-1, -1))


def two_sum(a, b):
    total = a + b
    virtual = total - a
    return total, (a - (total - virtual)) + (b - virtual)


def split(a):
    scaled = a * 4097.0
    high = scaled - (scaled - a)
    return high, a - high


def two_product(a, b):
    product = a * b
    a_high, a_low = split(a)
    b_high, b_low = split(b)
    error = ((a_high * b_high - product) + a_high * b_low + a_low * b_high) + a_low * b_low
    return product, error


def pair_add(a, b):
    total, error = two_sum(a[0], b[0])
    return total, error + (a[1] + b[1])


def renormal(a):
    total = a[0] + a[1]
    return total, a[1] - (total - a[0])


def tree(parts):
    while len(parts) > 1:
        rest = parts[len(parts) // 2 * 2 :]
        parts = [pair_add(parts[i], parts[i + 1]) for i in range(0, len(parts) - 1, 2)] + rest
    return parts[0]


AT_Z, AT_X, AT_Y, AT_BEHIND = range(4)


def sum_pairs(parts):
    while len(parts) > 1:
        rest = parts[len(parts) // 2 * 2 :]
        added = []
        for i in range(0, len(parts) - 1, 2):
            total, error = two_sum(parts[i][0], parts[i + 1][0])
            added.append((total, error + (parts[i][1] + parts[i + 1][1])))
        parts = added + rest
    return parts[0]


def sum_rows(tiles):
    zero = jnp.zeros_like(tiles[0])
    total = sum_pairs([(tile, zero) for tile in tiles])
    shift = SUBLANES // 2
    while shift:
        total = pair_add(total, tuple(pltpu.roll(piece, shift, 0) for piece in total))
        shift //= 2
    return total


def fold(total):
    lead, minor = total
    return renormal((lead, minor + pltpu.roll(lead + minor, LANES // 2, 1)))


def wrap(high, low):
    lane = lax.broadcasted_iota(jnp.int32, high.shape, 1)
    return jnp.where(lane < LANES // 2, high, pltpu.roll(low, LANES // 2, 1))


def plan(depth):
    return (4,) * (depth // 4)


def stages_of(count_y, count_z):
    if count_y * count_z <= 64:
        return (("py", "pz"),)
    return (("pz",), ("py",))


def first_pair(column):
    return column * (column + 1) // 2


def kernel(
    groups,
    count_y,
    count_z,
    root_cells,
    start_hbm,
    x_hbm,
    y_hbm,
    z_hbm,
    shifts,
    field,
    triangle,
    coef,
    partial,
    row_source,
    *rest,
):
    stages = stages_of(count_y, count_z)
    row_buffers = rest[: len(stages)]
    load_sem, send_sem, recv_sem, coef_send, coef_recv, row_send, row_recv = rest[len(stages) :]
    depth = shifts.shape[0]
    count = depth + 1
    rows_y, rows_z, length = start_hbm.shape
    span_y, span_z = field.shape[1:3]
    half_y, half_z = (span_y - rows_y) // 2, (span_z - rows_z) // 2
    padded = triangle.shape[0]
    sizes = {"py": count_y, "pz": count_z}
    me = {"py": lax.axis_index("py"), "pz": lax.axis_index("pz")}
    me_y, me_z = me["py"], me["pz"]
    most = max(groups)

    has = []
    comes = []
    target = []
    for dy, dz in WAYS:
        ahead, behind = [], []
        for step, at, size in ((dy, me_y, count_y), (dz, me_z, count_z)):
            if step:
                up, down = at < size - 1, at > 0
                ahead.append(up if step > 0 else down)
                behind.append(down if step > 0 else up)
        has.append(functools.reduce(jnp.logical_and, ahead))
        comes.append(functools.reduce(jnp.logical_and, behind))
        target.append({"py": me_y + dy, "pz": me_z + dz})

    barrier = pltpu.get_barrier_semaphore()
    if len(stages) == 1:
        expected = count_y * count_z - 1

        def greet(away, carry):
            other = lax.rem(me_y * count_z + me_z + away, count_y * count_z)
            pl.semaphore_signal(
                barrier,
                inc=1,
                device_id={"py": lax.div(other, count_z), "pz": lax.rem(other, count_z)},
                device_id_type=MESH,
            )
            return carry

        lax.fori_loop(1, count_y * count_z, greet, 0)
    else:
        expected = count_y + count_z - 2
        for axis, size in sizes.items():
            def greet(away, carry):
                pl.semaphore_signal(
                    barrier, inc=1, device_id={axis: lax.rem(me[axis] + away, size)}, device_id_type=MESH
                )
                return carry

            lax.fori_loop(1, size, greet, 0)
        for way in range(4, 8):
            pl.when(has[way])(
                lambda way=way: pl.semaphore_signal(
                    barrier, inc=1, device_id=target[way], device_id_type=MESH
                )
            )
            expected = expected + jnp.where(comes[way], 1, 0)

    own = (pl.ds(half_y, rows_y), pl.ds(0, rows_z))
    loads = [
        pltpu.make_async_copy(source, place.at[own], load_sem.at[i])
        for i, (source, place) in enumerate(
            (
                (start_hbm, field.at[0]),
                (z_hbm, coef.at[AT_Z]),
                (y_hbm, coef.at[AT_Y]),
                (x_hbm, coef.at[AT_X]),
            )
        )
    ]
    for load in loads:
        load.start()

    def ends_y(step, first, last):
        if step > 0:
            return pl.ds(half_y + rows_y - last, last - first), pl.ds(half_y - last, last - first)
        if step < 0:
            return pl.ds(half_y + first, last - first), pl.ds(half_y + rows_y + first, last - first)
        return pl.ds(half_y, rows_y), pl.ds(half_y, rows_y)

    def ends_z(step, first, last):
        if step > 0:
            return pl.ds(rows_z - last, last - first), pl.ds(span_z - last, last - first)
        if step < 0:
            return pl.ds(first, last - first), pl.ds(rows_z + first, last - first)
        return pl.ds(0, rows_z), pl.ds(0, rows_z)

    def copy(array, which, way, y_band, z_band, sends, recvs, index):
        dy, dz = WAYS[way]
        from_y, to_y = ends_y(dy, *y_band)
        from_z, to_z = ends_z(dz, *z_band)
        return way, pltpu.make_async_remote_copy(
            src_ref=array.at[which, from_y, from_z],
            dst_ref=array.at[which, to_y, to_z],
            send_sem=sends.at[index],
            recv_sem=recvs.at[index],
            device_id=target[way],
            device_id_type=MESH,
        )

    def start_all(copies):
        for way, each in copies:
            pl.when(has[way])(lambda each=each: each.start())

    def arrive_all(copies):
        for way, each in copies:
            pl.when(comes[way])(lambda each=each: each.wait_recv())

    def leave_all(copies):
        for way, each in copies:
            pl.when(has[way])(lambda each=each: each.wait_send())

    def field_copies(group):
        slot, reach = sum(groups[:group]), groups[group]
        bands = [(0, reach if way < 4 else reach - 1) for way in range(8 if reach > 1 else 4)]
        return [
            copy(field, slot, way, band, band, send_sem, recv_sem, group * 8 + way)
            for way, band in enumerate(bands)
        ]

    coef_parts = []

    def coef_band(before, after):
        copies = []

        def add(which, way, y_band, z_band):
            if y_band[1] > y_band[0] and z_band[1] > z_band[0]:
                index = len(coef_parts)
                coef_parts.append(index)
                copies.append(copy(coef, which, way, y_band, z_band, coef_send, coef_recv, index))

        for way, (dy, dz) in enumerate(WAYS):
            if way < 4:
                low = (max(before - 1, 0), after - 1)
                if dy + dz < 0:
                    add(pl.ds(0, 3), way, low, low)
                else:
                    add(AT_Y if dy else AT_Z, way, (before, after), (before, after))
                    add(pl.ds(AT_Z if dy else AT_X, 2), way, low, low)
            else:
                less = 2 if dy < 0 and dz < 0 else 1
                old, new = max(before - less, 0), max(after - less, 0)
                add(pl.ds(0, 3), way, (0, old), (old, new))
                add(pl.ds(0, 3), way, (old, new), (0, new))
        return copies

    fields = [field_copies(group) for group in range(len(groups))]
    early, late = coef_band(0, groups[0]), coef_band(groups[0], most)

    for load in loads:
        load.wait()
    pl.semaphore_wait(barrier, expected)
    start_all(fields[0])
    start_all(early)
    start_all(late)

    def clear(block_y, block_z):
        shape = (block_y[1], block_z[1], length)
        where = (pl.ds(*block_y), pl.ds(*block_z))

        def one(piece, carry):
            coef[(piece, *where)] = jnp.zeros(shape, jnp.float32)
            return carry

        lax.fori_loop(0, 3, one, 0)
        for group in range(len(groups)):
            field[(sum(groups[:group]), *where)] = jnp.zeros(shape, jnp.float32)

    pl.when(me_y == 0)(lambda: clear((0, half_y), (0, span_z)))
    pl.when(me_y == count_y - 1)(lambda: clear((half_y + rows_y, half_y), (0, span_z)))
    pl.when(me_z == 0)(lambda: clear((0, span_y), (rows_z + half_z, half_z)))
    pl.when(me_z == count_z - 1)(lambda: clear((0, span_y), (rows_z, half_z)))

    pieces = range(length // LANES)
    last_piece = length // LANES - 1
    lane = lax.broadcasted_iota(jnp.int32, (rows_z, LANES), 1)
    sub = lax.broadcasted_iota(jnp.int32, (rows_z, LANES), 0)
    right_edge, left_edge = lane == LANES - 1, lane == 0
    top_row, bottom_row = sub == rows_z - 1, sub == 0
    inside_z = jnp.where(
        sub < half_z,
        jnp.where(me_z < count_z - 1, 1.0, 0.0),
        jnp.where(me_z > 0, 1.0, 0.0),
    )
    scale_below = jnp.where(me_y > 0, step_scale, 0.0)
    scale_above = jnp.where(me_y < count_y - 1, step_scale, 0.0)

    def shifted(rows):
        ahead = [pltpu.roll(row, LANES - 1, 1) for row in rows]
        behind = [pltpu.roll(row, 1, 1) for row in rows]
        return (
            [jnp.where(right_edge, ahead[x + 1] if x < last_piece else 0.0, ahead[x]) for x in pieces],
            [jnp.where(left_edge, behind[x - 1] if x else 0.0, behind[x]) for x in pieces],
        )

    def turn_x(first, last, tiles):
        def row(y, carry):
            for tile in tiles:
                where = [(y, pl.ds(tile * rows_z, rows_z), pl.ds(x * LANES, LANES)) for x in pieces]
                for at, behind in zip(where, shifted([coef[(AT_X, *at)] for at in where])[1]):
                    coef[(AT_BEHIND, *at)] = behind
            return carry

        lax.fori_loop(first, last, row, 0, unroll=last - first)

    def level(group, step):
        slot = sum(groups[:group]) + step
        left = groups[group] - step - 1
        shift = shifts[slot]
        tiles = (0, 1) if left else (0,)

        def at(tile, x):
            return pl.ds(tile * rows_z, rows_z), pl.ds(x * LANES, LANES)

        def value(y, tile, x):
            return field[(slot, y, *at(tile, x))]

        def factor(which, y, tile, x):
            return coef[(which, y, *at(tile, x))]

        def edge(array, which, y, z, x):
            return array[which, y, pl.ds(z, 1), pl.ds(x * LANES, LANES)]

        def part_z(y, x):
            if left:
                rows = [value(y, tile, x) for tile in tiles]
                turned = [pltpu.roll(row, rows_z - 1, 0) for row in rows]
                flux = [
                    factor(AT_Z, y, tile, x)
                    * (rows[tile] - jnp.where(top_row, turned[1 - tile], turned[tile]))
                    for tile in tiles
                ]
                turned = [pltpu.roll(each, 1, 0) for each in flux]
                return [
                    flux[tile] - jnp.where(bottom_row, turned[1 - tile], turned[tile]) for tile in tiles
                ]
            row = value(y, 0, x)
            up = jnp.where(top_row, edge(field, slot, y, rows_z, x), pltpu.roll(row, rows_z - 1, 0))
            flux = factor(AT_Z, y, 0, x) * (row - up)
            below = edge(coef, AT_Z, y, span_z - 1, x) * (edge(field, slot, y, span_z - 1, x) - row[0:1, :])
            return [flux - jnp.where(bottom_row, below, pltpu.roll(flux, 1, 0))]

        def part_x(y, tile):
            rows = [value(y, tile, x) for x in pieces]
            ahead, behind = shifted(rows)
            return [
                factor(AT_X, y, tile, x) * (rows[x] - ahead[x])
                + factor(AT_BEHIND, y, tile, x) * (rows[x] - behind[x])
                for x in pieces
            ]

        def flux_y(y, tile, x):
            return factor(AT_Y, y, tile, x) * (value(y, tile, x) - value(y + 1, tile, x))

        first, last = half_y - left, half_y + rows_y + left

        def rows_of(at_chunk, carried):
            start = first + at_chunk * chunk
            along_x = [[part_x(start + i, tile) for tile in tiles] for i in range(chunk)]
            ready = []
            for i in range(chunk):
                y = start + i
                scale = step_scale
                if left:
                    scale = jnp.where(
                        y < half_y, scale_below, jnp.where(y < half_y + rows_y, step_scale, scale_above)
                    )
                along_z = [part_z(y, x) for x in pieces]
                above = []
                for tile in tiles:
                    scale_tile = scale * inside_z if tile else scale
                    for x in pieces:
                        flux = flux_y(y, tile, x)
                        change = (flux - carried[len(above)]) - shift * value(y, tile, x)
                        fresh = (along_x[i][tile][x] + along_z[x][tile]) + change
                        ready.append(((slot + 1, y, *at(tile, x)), fresh * scale_tile))
                        above.append(flux)
                carried = above
            for place, fresh in ready:
                field[place] = fresh
            return tuple(carried)

        chunk = last - first
        below = tuple(flux_y(first - 1, tile, x) for tile in tiles for x in pieces)
        lax.fori_loop(0, (last - first) // chunk, rows_of, below)

    def gram(columns):
        pairs = [(i, j) for j in columns for i in range(j + 1)]

        def plane(y, totals):
            totals = list(totals)
            for x in range(0, length, LANES):
                pieces = [field[i, half_y + y, pl.ds(0, rows_z), pl.ds(x, LANES)] for i in range(max(columns) + 1)]
                for p, (i, j) in enumerate(pairs):
                    totals[p] = totals[p] + pieces[i] * pieces[j]
            return tuple(totals)

        zero = jnp.zeros((SUBLANES, LANES), jnp.float32)
        totals = lax.fori_loop(0, rows_y, plane, (zero,) * len(pairs))
        for (i, j), total in zip(pairs, totals):
            partial[pl.ds((first_pair(j) + i) * SUBLANES, SUBLANES), :] = total

    pairs = first_pair(count)
    many = partial.shape[0] // SUBLANES
    for at in range(pairs, many):
        partial[pl.ds(at * SUBLANES, SUBLANES), :] = jnp.zeros((SUBLANES, LANES), jnp.float32)

    turn_x(half_y, half_y + rows_y, (0,))
    for group, applications in enumerate(groups):
        if group == 1:
            arrive_all(late)
        if group:
            start_all(fields[group])
            gram(range(0 if group == 1 else sum(groups[: group - 1]) + 1, sum(groups[:group]) + 1))
        arrive_all(fields[group])
        if group == 0:
            arrive_all(early)
        if group == 0:
            turn_x(half_y - (most - 1), half_y, (0, 1))
            turn_x(half_y, half_y + rows_y, (1,))
            turn_x(half_y + rows_y, half_y + rows_y + most - 1, (0, 1))
        for step in range(applications):
            level(group, step)
    gram(range(sum(groups[:-1]) + 1, count))

    high, low = sum_pairs(
        [
            (partial[pl.ds(s, many, stride=SUBLANES), :], jnp.zeros((many, LANES), jnp.float32))
            for s in range(SUBLANES)
        ]
    )
    fill = jnp.zeros((LANES // 2 - many, LANES), jnp.float32)
    turned = jnp.concatenate([high, fill, low, fill], axis=0).T
    total = fold(sum_rows([turned[y : y + SUBLANES] for y in range(0, LANES, SUBLANES)]))
    for stage, axes in enumerate(stages):
        buffer = row_buffers[stage]
        size = math.prod(sizes[axis] for axis in axes)
        index = functools.reduce(lambda at, axis: at * sizes[axis] + me[axis], axes, 0)
        row_source[stage] = wrap(*total)
        if buffer.shape[0] > size:
            buffer[pl.ds(size, buffer.shape[0] - size), :] = jnp.zeros(
                (buffer.shape[0] - size, LANES), jnp.float32
            )

        def send(away, carry):
            other = lax.rem(index + away, size)
            device = {}
            for axis in reversed(axes):
                device[axis] = lax.rem(other, sizes[axis])
                other = lax.div(other, sizes[axis])
            pltpu.make_async_remote_copy(
                src_ref=row_source.at[stage, pl.ds(0, 1)],
                dst_ref=buffer.at[pl.ds(index, 1)],
                send_sem=row_send.at[stage],
                recv_sem=row_recv.at[stage],
                device_id=device,
                device_id_type=MESH,
            ).start()
            return carry

        lax.fori_loop(1, size, send, 0)
        buffer[pl.ds(index, 1), :] = row_source[stage, pl.ds(0, 1), :]
        if stage == 0:
            for copies in (*fields, early, late):
                leave_all(copies)
        others = buffer.at[pl.ds(0, size - 1)]
        pltpu.make_async_copy(others, others, row_recv.at[stage]).wait()
        pltpu.make_async_copy(others, others, row_send.at[stage]).wait()
        rows = [buffer[pl.ds(y, SUBLANES), :] for y in range(0, buffer.shape[0], SUBLANES)]
        total = fold(sum_rows(rows))

    square_sub = lax.broadcasted_iota(jnp.int32, (padded, LANES), 0)
    square_lane = lax.broadcasted_iota(jnp.int32, (padded, LANES), 1)
    zero = jnp.zeros((padded, LANES), jnp.float32)
    lower = []
    for piece in total:
        piece = jnp.concatenate([piece] * (padded // SUBLANES), axis=0)
        square = zero
        for column in range(count):
            at = first_pair(column)
            moved = pltpu.roll(piece, LANES - at, 1) if at else piece
            square = jnp.where(jnp.logical_and(square_sub == column, square_lane <= column), moved, square)
        lower.append(square)
    fill = jnp.zeros((LANES - 2 * padded, LANES), jnp.float32)
    turned = jnp.concatenate([*lower, fill], axis=0).T[:padded]
    g_high = jnp.where(square_lane < square_sub, lower[0], turned)
    g_low = jnp.where(square_lane < square_sub, lower[1], pltpu.roll(turned, LANES - padded, 1))

    tri = zero
    row_lane = lax.broadcasted_iota(jnp.int32, (1, LANES), 1)
    for k in range(count):
        row_high, row_low = g_high[k : k + 1, :], g_low[k : k + 1, :]
        d_high = jnp.broadcast_to(row_high[:, k : k + 1], (1, LANES))
        d_low = jnp.broadcast_to(row_low[:, k : k + 1], (1, LANES))
        within = jnp.logical_and(row_lane >= k, row_lane < count)
        factor = jnp.where(within, row_high / jnp.sqrt(d_high) / root_cells, 0.0)
        tri = jnp.where(square_sub == k, factor, tri)
        if k == count - 1:
            break
        inverse = 1.0 / d_high
        lead = row_high * inverse
        product, error = two_product(lead, d_high)
        minor = (((row_high - product) - error) + (row_low - lead * d_low)) * inverse
        col_high = jnp.broadcast_to(g_high[:, k : k + 1], (padded, LANES))
        col_low = jnp.broadcast_to(g_low[:, k : k + 1], (padded, LANES))
        lead = jnp.broadcast_to(lead, (padded, LANES))
        minor = jnp.broadcast_to(minor, (padded, LANES))
        product, error = two_product(col_high, lead)
        error = error + (col_high * minor + col_low * lead)
        total, rest_of = two_sum(g_high, -product)
        g_high, g_low = renormal((total, rest_of + (g_low - error)))
    triangle[...] = tri


def substitute(basis, factor, out, triangle, splat):
    count, rows_y, rows_z, length = out.shape
    first = pl.program_id(0) * rows_y + (basis.shape[1] - rows_y * pl.num_programs(0)) // 2

    @pl.when(pl.program_id(0) == 0)
    def _():
        tri = factor[...]
        triangle[...] = tri[:count, :count]
        for k in range(count):
            for i in range(k, count):
                value = jnp.broadcast_to(tri[k : k + 1, i : i + 1], (SUBLANES, LANES))
                splat[k * count + i] = 1.0 / value if i == k else value

    def plane(y, carry):
        for x in range(0, length, LANES):
            solved = []
            for i in range(count):
                value = basis[i, first + y, pl.ds(0, rows_z), x : x + LANES]
                for k in range(i):
                    value = value - splat[k * count + i] * solved[k]
                value = value * splat[i * count + i]
                out[i, y, :, x : x + LANES] = value
                solved.append(value)
        return carry

    lax.fori_loop(0, rows_y, plane, 0)


def on_device(start, coef_x, coef_y, coef_z, shifts):
    rows_y, rows_z, length = start.shape
    depth = shifts.shape[0]
    count = depth + 1
    padded = (count + SUBLANES - 1) // SUBLANES * SUBLANES
    count_y, count_z = lax.axis_size("py"), lax.axis_size("pz")
    cells = length * rows_y * rows_z * count_y * count_z
    groups = plan(depth)
    span_y, span_z = rows_y + 8, rows_z + 8
    stages = stages_of(count_y, count_z)
    sizes = {"py": count_y, "pz": count_z}
    members = [math.prod(sizes[axis] for axis in axes) for axes in stages]
    whole = pl.BlockSpec(memory_space=pltpu.VMEM)
    many = (first_pair(count) + SUBLANES - 1) // SUBLANES * SUBLANES
    pltpu_f32 = lambda *shape: pltpu.VMEM(shape, jnp.float32)
    dma = pltpu.SemaphoreType.DMA
    vmem_limit = 2**26 - 4 * (count * span_y * span_z * length) - 2**18
    anywhere = pl.BlockSpec(memory_space=pl.ANY)
    basis, factor = pl.pallas_call(
        functools.partial(kernel, groups, count_y, count_z, math.sqrt(cells)),
        out_shape=(
            pltpu_f32(count, span_y, span_z, length),
            pltpu_f32(padded, LANES),
        ),
        in_specs=[anywhere] * 4 + [pl.BlockSpec(memory_space=pltpu.SMEM)],
        out_specs=(whole, whole),
        scratch_shapes=[
            pltpu_f32(4, span_y, span_z, length),
            pltpu_f32(many * SUBLANES, LANES),
            pltpu_f32(len(stages), SUBLANES, LANES),
            *[pltpu_f32((n + SUBLANES - 1) // SUBLANES * SUBLANES, LANES) for n in members],
            dma((4,)),
            dma((len(groups) * 8,)),
            dma((len(groups) * 8,)),
            dma((32,)),
            dma((32,)),
            dma((len(stages),)),
            dma((len(stages),)),
        ],
        compiler_params=pltpu.CompilerParams(
            collective_id=0, has_side_effects=True, vmem_limit_bytes=vmem_limit
        ),
    )(start, coef_x, coef_y, coef_z, shifts)
    basis = pltpu.with_memory_space_constraint(basis, pltpu.VMEM)
    factor = pltpu.with_memory_space_constraint(factor, pltpu.VMEM)
    block = (count, max(1, rows_y // 4), rows_z, length)
    planes = pl.BlockSpec(block, lambda i: (0, i, 0, 0))
    return pl.pallas_call(
        substitute,
        grid=(rows_y // block[1],),
        out_shape=(
            jax.ShapeDtypeStruct((count, rows_y, rows_z, length), jnp.float32),
            jax.ShapeDtypeStruct((count, count), jnp.float32),
        ),
        in_specs=[whole, whole],
        out_specs=(planes, pl.BlockSpec((count, count), lambda i: (0, 0))),
        scratch_shapes=[pltpu_f32(count * count, SUBLANES, LANES)],
        compiler_params=pltpu.CompilerParams(vmem_limit_bytes=vmem_limit),
    )(basis, factor)


def solution(mesh):
    placed = (
        P("py", "pz", None),
        P("py", "pz", None),
        P("py", "pz", None),
        P("py", "pz", None),
        P(),
    )
    return jax.shard_map(
        on_device,
        mesh=mesh,
        in_specs=placed,
        out_specs=(P(None, "py", "pz", None), P()),
        check_vma=False,
    )
```

```python
import functools
import math

import jax
import jax.numpy as jnp
from jax import lax
from jax.experimental import pallas as pl
from jax.experimental.pallas import tpu as pltpu
from jax.sharding import PartitionSpec as P

step_scale = 0.125
MESH = pl.DeviceIdType.MESH
LANES = 128
SUBLANES = 8
WAYS = ((1, 0), (-1, 0), (0, 1), (0, -1), (1, 1), (1, -1), (-1, 1), (-1, -1))


def two_sum(a, b):
    total = a + b
    virtual = total - a
    return total, (a - (total - virtual)) + (b - virtual)


def split(a):
    scaled = a * 4097.0
    high = scaled - (scaled - a)
    return high, a - high


def two_product(a, b):
    product = a * b
    a_high, a_low = split(a)
    b_high, b_low = split(b)
    error = ((a_high * b_high - product) + a_high * b_low + a_low * b_high) + a_low * b_low
    return product, error


def pair_add(a, b):
    total, error = two_sum(a[0], b[0])
    return total, error + (a[1] + b[1])


def renormal(a):
    total = a[0] + a[1]
    return total, a[1] - (total - a[0])


def tree(parts):
    while len(parts) > 1:
        rest = parts[len(parts) // 2 * 2 :]
        parts = [pair_add(parts[i], parts[i + 1]) for i in range(0, len(parts) - 1, 2)] + rest
    return parts[0]


AT_Z, AT_X, AT_Y, AT_BEHIND = range(4)


def sum_pairs(parts):
    while len(parts) > 1:
        rest = parts[len(parts) // 2 * 2 :]
        added = []
        for i in range(0, len(parts) - 1, 2):
            total, error = two_sum(parts[i][0], parts[i + 1][0])
            added.append((total, error + (parts[i][1] + parts[i + 1][1])))
        parts = added + rest
    return parts[0]


def sum_rows(tiles):
    zero = jnp.zeros_like(tiles[0])
    total = sum_pairs([(tile, zero) for tile in tiles])
    shift = SUBLANES // 2
    while shift:
        total = pair_add(total, tuple(pltpu.roll(piece, shift, 0) for piece in total))
        shift //= 2
    return total


def fold(total):
    lead, minor = total
    return renormal((lead, minor + pltpu.roll(lead + minor, LANES // 2, 1)))


def wrap(high, low):
    lane = lax.broadcasted_iota(jnp.int32, high.shape, 1)
    return jnp.where(lane < LANES // 2, high, pltpu.roll(low, LANES // 2, 1))


def plan(depth):
    first = depth % 3 or 3
    return (first,) + (3,) * ((depth - first) // 3)


def stages_of(count_y, count_z):
    if count_y * count_z <= 64:
        return (("py", "pz"),)
    return (("pz",), ("py",))


def first_pair(column):
    return column * (column + 1) // 2


def kernel(
    groups,
    count_y,
    count_z,
    root_cells,
    start_hbm,
    x_hbm,
    y_hbm,
    z_hbm,
    shifts,
    field,
    triangle,
    splat,
    coef,
    coef_late,
    partial,
    row_source,
    *rest,
):
    stages = stages_of(count_y, count_z)
    row_buffers = rest[: len(stages)]
    load_sem, send_sem, recv_sem, coef_send, coef_recv, row_send, row_recv = rest[len(stages) :]
    depth = shifts.shape[0]
    count = depth + 1
    rows_y, rows_z, length = start_hbm.shape
    span_y, span_z = field.shape[1:3]
    half_y, half_z = (span_y - rows_y) // 2, (span_z - rows_z) // 2
    padded = triangle.shape[0]
    sizes = {"py": count_y, "pz": count_z}
    me = {"py": lax.axis_index("py"), "pz": lax.axis_index("pz")}
    me_y, me_z = me["py"], me["pz"]
    most = max(groups)

    has = []
    comes = []
    target = []
    for dy, dz in WAYS:
        ahead, behind = [], []
        for step, at, size in ((dy, me_y, count_y), (dz, me_z, count_z)):
            if step:
                up, down = at < size - 1, at > 0
                ahead.append(up if step > 0 else down)
                behind.append(down if step > 0 else up)
        has.append(functools.reduce(jnp.logical_and, ahead))
        comes.append(functools.reduce(jnp.logical_and, behind))
        target.append({"py": me_y + dy, "pz": me_z + dz})

    barrier = pltpu.get_barrier_semaphore()
    if len(stages) == 1:
        expected = count_y * count_z - 1

        def greet(away, carry):
            other = lax.rem(me_y * count_z + me_z + away, count_y * count_z)
            pl.semaphore_signal(
                barrier,
                inc=1,
                device_id={"py": lax.div(other, count_z), "pz": lax.rem(other, count_z)},
                device_id_type=MESH,
            )
            return carry

        lax.fori_loop(1, count_y * count_z, greet, 0)
    else:
        expected = count_y + count_z - 2
        for axis, size in sizes.items():
            def greet(away, carry):
                pl.semaphore_signal(
                    barrier, inc=1, device_id={axis: lax.rem(me[axis] + away, size)}, device_id_type=MESH
                )
                return carry

            lax.fori_loop(1, size, greet, 0)
        for way in range(4, 8):
            pl.when(has[way])(
                lambda way=way: pl.semaphore_signal(
                    barrier, inc=1, device_id=target[way], device_id_type=MESH
                )
            )
            expected = expected + jnp.where(comes[way], 1, 0)

    own = (pl.ds(half_y, rows_y), pl.ds(0, rows_z))
    loads = [
        pltpu.make_async_copy(source, place.at[own], load_sem.at[i])
        for i, (source, place) in enumerate(
            (
                (start_hbm, field.at[0]),
                (z_hbm, coef.at[AT_Z]),
                (y_hbm, coef.at[AT_Y]),
                (x_hbm, coef.at[AT_X]),
            )
        )
    ]
    for load in loads:
        load.start()

    def ends_y(step, first, last):
        if step > 0:
            return pl.ds(half_y + rows_y - last, last - first), pl.ds(half_y - last, last - first)
        if step < 0:
            return pl.ds(half_y + first, last - first), pl.ds(half_y + rows_y + first, last - first)
        return pl.ds(half_y, rows_y), pl.ds(half_y, rows_y)

    def ends_z(step, first, last):
        if step > 0:
            return pl.ds(rows_z - last, last - first), pl.ds(span_z - last, last - first)
        if step < 0:
            return pl.ds(first, last - first), pl.ds(rows_z + first, last - first)
        return pl.ds(0, rows_z), pl.ds(0, rows_z)

    def copy(array, which, way, y_band, z_band, sends, recvs, index, place=None):
        dy, dz = WAYS[way]
        from_y, to_y = ends_y(dy, *y_band)
        from_z, to_z = ends_z(dz, *z_band)
        return way, pltpu.make_async_remote_copy(
            src_ref=array.at[which, from_y, from_z],
            dst_ref=(array if place is None else place).at[which, to_y, to_z],
            send_sem=sends.at[index],
            recv_sem=recvs.at[index],
            device_id=target[way],
            device_id_type=MESH,
        )

    def start_all(copies):
        for way, each in copies:
            pl.when(has[way])(lambda each=each: each.start())

    def arrive_all(copies):
        for way, each in copies:
            pl.when(comes[way])(lambda each=each: each.wait_recv())

    def leave_all(copies):
        for way, each in copies:
            pl.when(has[way])(lambda each=each: each.wait_send())

    def field_copies(group):
        slot, reach = sum(groups[:group]), groups[group]
        bands = [(0, reach if way < 4 else reach - 1) for way in range(8 if reach > 1 else 4)]
        return [
            copy(field, slot, way, band, band, send_sem, recv_sem, group * 8 + way)
            for way, band in enumerate(bands)
        ]

    coef_parts = []

    def coef_band(before, after):
        copies = []

        def add(which, way, y_band, z_band, place=None):
            if y_band[1] > y_band[0] and z_band[1] > z_band[0]:
                index = len(coef_parts)
                coef_parts.append(index)
                copies.append(copy(coef, which, way, y_band, z_band, coef_send, coef_recv, index, place))

        for way, (dy, dz) in enumerate(WAYS):
            if way < 2:
                low = (max(before - 1, 0), after - 1)
                if dy < 0:
                    add(pl.ds(0, 3), way, low, low)
                else:
                    add(AT_Y, way, (before, after), (0, 1))
                    add(pl.ds(AT_Z, 2), way, low, (0, 1))
                continue
            place = coef_late if before else coef
            if way < 4:
                low = (0, after - 1)
                if dz < 0:
                    add(pl.ds(0, 3), way, low, low, place)
                else:
                    add(AT_Z, way, (0, 1), (0, after), place)
                    add(pl.ds(AT_X, 2), way, (0, 1), low, place)
            else:
                band = (0, max(after - (2 if dy < 0 and dz < 0 else 1), 0))
                add(pl.ds(0, 3), way, band, band, place)
        return copies

    fields = [field_copies(group) for group in range(len(groups))]
    early, late = coef_band(0, groups[0]), coef_band(groups[0], most) if most > groups[0] else []

    for load in loads:
        load.wait()
    pl.semaphore_wait(barrier, expected)
    start_all(fields[0])
    start_all(early)
    start_all(late)

    def clear(block_y, block_z):
        shape = (block_y[1], block_z[1], length)
        where = (pl.ds(*block_y), pl.ds(*block_z))

        def one(piece, carry):
            coef[(piece, *where)] = jnp.zeros(shape, jnp.float32)
            coef_late[(piece, *where)] = jnp.zeros(shape, jnp.float32)
            return carry

        lax.fori_loop(0, 3, one, 0)
        for group in range(len(groups)):
            field[(sum(groups[:group]), *where)] = jnp.zeros(shape, jnp.float32)

    pl.when(me_y == 0)(lambda: clear((0, half_y), (0, span_z)))
    pl.when(me_y == count_y - 1)(lambda: clear((half_y + rows_y, half_y), (0, span_z)))
    pl.when(me_z == 0)(lambda: clear((0, span_y), (rows_z + half_z, half_z)))
    pl.when(me_z == count_z - 1)(lambda: clear((0, span_y), (rows_z, half_z)))

    pieces = range(length // LANES)
    last_piece = length // LANES - 1
    lane = lax.broadcasted_iota(jnp.int32, (rows_z, LANES), 1)
    sub = lax.broadcasted_iota(jnp.int32, (rows_z, LANES), 0)
    right_edge, left_edge = lane == LANES - 1, lane == 0
    top_row, bottom_row = sub == rows_z - 1, sub == 0
    inside_z = jnp.where(
        sub < half_z,
        jnp.where(me_z < count_z - 1, 1.0, 0.0),
        jnp.where(me_z > 0, 1.0, 0.0),
    )
    scale_below = jnp.where(me_y > 0, step_scale, 0.0)
    scale_above = jnp.where(me_y < count_y - 1, step_scale, 0.0)

    def shifted(rows):
        ahead = [pltpu.roll(row, LANES - 1, 1) for row in rows]
        behind = [pltpu.roll(row, 1, 1) for row in rows]
        return (
            [jnp.where(right_edge, ahead[x + 1] if x < last_piece else 0.0, ahead[x]) for x in pieces],
            [jnp.where(left_edge, behind[x - 1] if x else 0.0, behind[x]) for x in pieces],
        )

    def turn_x(array, first, last, tile):
        for y in range(first, last):
            where = [(y, pl.ds(tile * rows_z, rows_z), pl.ds(x * LANES, LANES)) for x in pieces]
            for at, behind in zip(where, shifted([array[(AT_X, *at)] for at in where])[1]):
                array[(AT_BEHIND, *at)] = behind

    def level(group, step):
        slot = sum(groups[:group]) + step
        left = groups[group] - step - 1
        shift = shifts[slot]
        tiles = (0, 1) if left else (0,)

        def at(tile, x):
            return pl.ds(tile * rows_z, rows_z), pl.ds(x * LANES, LANES)

        def value(y, tile, x):
            return field[(slot, y, *at(tile, x))]

        beyond = coef_late if group else coef

        def factor(which, y, tile, x):
            return (beyond if tile else coef)[(which, y, *at(tile, x))]

        def edge(array, which, y, z, x):
            return array[which, y, pl.ds(z, 1), pl.ds(x * LANES, LANES)]

        def part_z(y, x, outer):
            if outer:
                rows = [value(y, tile, x) for tile in tiles]
                turned = [pltpu.roll(row, rows_z - 1, 0) for row in rows]
                flux = [
                    factor(AT_Z, y, tile, x)
                    * (rows[tile] - jnp.where(top_row, turned[1 - tile], turned[tile]))
                    for tile in tiles
                ]
                turned = [pltpu.roll(each, 1, 0) for each in flux]
                return [
                    flux[tile] - jnp.where(bottom_row, turned[1 - tile], turned[tile]) for tile in tiles
                ]
            row = value(y, 0, x)
            up = jnp.where(top_row, edge(field, slot, y, rows_z, x), pltpu.roll(row, rows_z - 1, 0))
            flux = factor(AT_Z, y, 0, x) * (row - up)
            below = edge(beyond, AT_Z, y, span_z - 1, x) * (edge(field, slot, y, span_z - 1, x) - row[0:1, :])
            return [flux - jnp.where(bottom_row, below, pltpu.roll(flux, 1, 0))]

        def part_x(y, tile):
            rows = [value(y, tile, x) for x in pieces]
            ahead, behind = shifted(rows)
            return [
                factor(AT_X, y, tile, x) * (rows[x] - ahead[x])
                + factor(AT_BEHIND, y, tile, x) * (rows[x] - behind[x])
                for x in pieces
            ]

        def flux_y(y, tile, x):
            return factor(AT_Y, y, tile, x) * (value(y, tile, x) - value(y + 1, tile, x))

        first, last = half_y - left, half_y + rows_y + left

        carried = {}
        for y in range(first, last):
            scale = step_scale if half_y <= y < half_y + rows_y else scale_below if y < half_y else scale_above
            here = tiles[:1] if left and y in (first, last - 1) else tiles
            along_x = [part_x(y, tile) for tile in here]
            along_z = [part_z(y, x, len(here) > 1) for x in pieces]
            for tile in here:
                scale_tile = scale * inside_z if tile else scale
                for x in pieces:
                    flux = flux_y(y, tile, x)
                    below = carried[tile, x] if (tile, x) in carried else flux_y(y - 1, tile, x)
                    change = (flux - below) - shift * value(y, tile, x)
                    fresh = (along_x[tile][x] + along_z[x][tile]) + change
                    field[(slot + 1, y, *at(tile, x))] = fresh * scale_tile
                    carried[tile, x] = flux

    def gram(columns):
        pairs = [(i, j) for j in columns for i in range(j + 1)]

        def plane(y, totals):
            totals = list(totals)
            for x in range(0, length, LANES):
                pieces = [field[i, half_y + y, pl.ds(0, rows_z), pl.ds(x, LANES)] for i in range(max(columns) + 1)]
                for p, (i, j) in enumerate(pairs):
                    totals[p] = totals[p] + pieces[i] * pieces[j]
            return tuple(totals)

        zero = jnp.zeros((SUBLANES, LANES), jnp.float32)
        totals = lax.fori_loop(0, rows_y, plane, (zero,) * len(pairs))
        for (i, j), total in zip(pairs, totals):
            partial[pl.ds((first_pair(j) + i) * SUBLANES, SUBLANES), :] = total

    pairs = first_pair(count)
    many = partial.shape[0] // SUBLANES
    for at in range(pairs, many):
        partial[pl.ds(at * SUBLANES, SUBLANES), :] = jnp.zeros((SUBLANES, LANES), jnp.float32)

    turn_x(coef, half_y, half_y + rows_y, 0)
    for group, applications in enumerate(groups):
        if group:
            start_all(fields[group])
        if group == 1:
            arrive_all(late)
            turn_x(coef, half_y - most + 1, half_y - groups[0] + 1, 0)
            turn_x(coef, half_y + rows_y + groups[0] - 1, half_y + rows_y + most - 1, 0)
            turn_x(coef_late, half_y - most + 2, half_y + rows_y + most - 2, 1)
        if group:
            gram(range(0 if group == 1 else sum(groups[: group - 1]) + 1, sum(groups[:group]) + 1))
        arrive_all(fields[group])
        if group == 0:
            arrive_all(early)
        if group == 0:
            reach = applications - 1
            turn_x(coef, half_y - reach, half_y, 0)
            turn_x(coef, half_y + rows_y, half_y + rows_y + reach, 0)
            turn_x(coef, half_y - reach + 1, half_y + rows_y + reach - 1, 1)
        for step in range(applications):
            level(group, step)
    gram(range(sum(groups[:-1]) + 1, count))

    high, low = sum_pairs(
        [
            (partial[pl.ds(s, many, stride=SUBLANES), :], jnp.zeros((many, LANES), jnp.float32))
            for s in range(SUBLANES)
        ]
    )
    fill = jnp.zeros((LANES // 2 - many, LANES), jnp.float32)
    turned = jnp.concatenate([high, fill, low, fill], axis=0).T
    total = fold(sum_rows([turned[y : y + SUBLANES] for y in range(0, LANES, SUBLANES)]))
    for stage, axes in enumerate(stages):
        buffer = row_buffers[stage]
        size = math.prod(sizes[axis] for axis in axes)
        index = functools.reduce(lambda at, axis: at * sizes[axis] + me[axis], axes, 0)
        row_source[stage] = wrap(*total)
        if buffer.shape[0] > size:
            buffer[pl.ds(size, buffer.shape[0] - size), :] = jnp.zeros(
                (buffer.shape[0] - size, LANES), jnp.float32
            )

        def send(away, carry):
            other = lax.rem(index + away, size)
            device = {}
            for axis in reversed(axes):
                device[axis] = lax.rem(other, sizes[axis])
                other = lax.div(other, sizes[axis])
            pltpu.make_async_remote_copy(
                src_ref=row_source.at[stage, pl.ds(0, 1)],
                dst_ref=buffer.at[pl.ds(index, 1)],
                send_sem=row_send.at[stage],
                recv_sem=row_recv.at[stage],
                device_id=device,
                device_id_type=MESH,
            ).start()
            return carry

        lax.fori_loop(1, size, send, 0)
        buffer[pl.ds(index, 1), :] = row_source[stage, pl.ds(0, 1), :]
        if stage == 0:
            for copies in (*fields, early, late):
                leave_all(copies)
        others = buffer.at[pl.ds(0, size - 1)]
        pltpu.make_async_copy(others, others, row_recv.at[stage]).wait()
        pltpu.make_async_copy(others, others, row_send.at[stage]).wait()
        rows = [buffer[pl.ds(y, SUBLANES), :] for y in range(0, buffer.shape[0], SUBLANES)]
        total = fold(sum_rows(rows))

    high, low = {}, {}
    for j in range(count):
        for i in range(j + 1):
            p = first_pair(j) + i
            high[i, j], low[i, j] = (
                jnp.broadcast_to(piece[:, p : p + 1], (SUBLANES, LANES)) for piece in total
            )
    square_sub = lax.broadcasted_iota(jnp.int32, (padded, LANES), 0)
    square_lane = lax.broadcasted_iota(jnp.int32, (padded, LANES), 1)
    tri = jnp.zeros((padded, LANES), jnp.float32)
    for k in range(count):
        for j in range(k, count):
            high[k, j], low[k, j] = renormal((high[k, j], low[k, j]))
        d_high, d_low = high[k, k], low[k, k]
        root = jnp.sqrt(d_high)
        for j in range(k, count):
            value = high[k, j] / root / root_cells
            splat[k * count + j] = 1.0 / value if j == k else value
            here = jnp.logical_and(square_sub == k, square_lane == j)
            tri = jnp.where(here, jnp.concatenate([value] * (padded // SUBLANES), axis=0), tri)
        inverse = 1.0 / d_high
        halves = {j: split(high[k, j]) for j in range(k, count)}
        for i in range(k + 1, count):
            lead = high[k, i] * inverse
            lead_high, lead_low = split(lead)

            def times(j):
                product = lead * high[k, j]
                big, small = halves[j]
                error = ((lead_high * big - product) + lead_high * small + lead_low * big) + lead_low * small
                return product, error

            product, error = times(k)
            minor = (((high[k, i] - product) - error) + (low[k, i] - lead * d_low)) * inverse
            for j in range(i, count):
                product, error = times(j)
                error = error + (high[k, j] * minor + low[k, j] * lead)
                rest_high, rest_low = two_sum(high[i, j], -product)
                high[i, j], low[i, j] = rest_high, rest_low + (low[i, j] - error)
    triangle[...] = tri


def substitute(basis, factor, splat, out, triangle):
    count, rows_y, rows_z, length = out.shape
    first = pl.program_id(0) * rows_y + (basis.shape[1] - rows_y * pl.num_programs(0)) // 2

    @pl.when(pl.program_id(0) == 0)
    def _():
        triangle[...] = factor[:count, :count]

    def plane(y, carry):
        for x in range(0, length, LANES):
            solved = []
            for i in range(count):
                value = basis[i, first + y, pl.ds(0, rows_z), x : x + LANES]
                for k in range(i):
                    value = value - splat[k * count + i] * solved[k]
                value = value * splat[i * count + i]
                out[i, y, :, x : x + LANES] = value
                solved.append(value)
        return carry

    lax.fori_loop(0, rows_y, plane, 0)


def on_device(start, coef_x, coef_y, coef_z, shifts):
    rows_y, rows_z, length = start.shape
    depth = shifts.shape[0]
    count = depth + 1
    padded = (count + SUBLANES - 1) // SUBLANES * SUBLANES
    count_y, count_z = lax.axis_size("py"), lax.axis_size("pz")
    cells = length * rows_y * rows_z * count_y * count_z
    groups = plan(depth)
    span_y, span_z = rows_y + 8, rows_z + 8
    stages = stages_of(count_y, count_z)
    sizes = {"py": count_y, "pz": count_z}
    members = [math.prod(sizes[axis] for axis in axes) for axes in stages]
    whole = pl.BlockSpec(memory_space=pltpu.VMEM)
    many = (first_pair(count) + SUBLANES - 1) // SUBLANES * SUBLANES
    pltpu_f32 = lambda *shape: pltpu.VMEM(shape, jnp.float32)
    dma = pltpu.SemaphoreType.DMA
    vmem_limit = 2**26 - 4 * (count * span_y * span_z * length) - 2**19
    anywhere = pl.BlockSpec(memory_space=pl.ANY)
    basis, factor, splat = pl.pallas_call(
        functools.partial(kernel, groups, count_y, count_z, math.sqrt(cells)),
        out_shape=(
            pltpu_f32(count, span_y, span_z, length),
            pltpu_f32(padded, LANES),
            pltpu_f32(count * count, SUBLANES, LANES),
        ),
        in_specs=[anywhere] * 4 + [pl.BlockSpec(memory_space=pltpu.SMEM)],
        out_specs=(whole, whole, whole),
        scratch_shapes=[
            pltpu_f32(4, span_y, span_z, length),
            pltpu_f32(4, span_y, span_z, length),
            pltpu_f32(many * SUBLANES, LANES),
            pltpu_f32(len(stages), SUBLANES, LANES),
            *[pltpu_f32((n + SUBLANES - 1) // SUBLANES * SUBLANES, LANES) for n in members],
            dma((4,)),
            dma((len(groups) * 8,)),
            dma((len(groups) * 8,)),
            dma((32,)),
            dma((32,)),
            dma((len(stages),)),
            dma((len(stages),)),
        ],
        compiler_params=pltpu.CompilerParams(
            collective_id=0, has_side_effects=True, vmem_limit_bytes=vmem_limit
        ),
    )(start, coef_x, coef_y, coef_z, shifts)
    basis = pltpu.with_memory_space_constraint(basis, pltpu.VMEM)
    factor = pltpu.with_memory_space_constraint(factor, pltpu.VMEM)
    splat = pltpu.with_memory_space_constraint(splat, pltpu.VMEM)
    block = (count, max(1, rows_y // 4), rows_z, length)
    planes = pl.BlockSpec(block, lambda i: (0, i, 0, 0))
    return pl.pallas_call(
        substitute,
        grid=(rows_y // block[1],),
        out_shape=(
            jax.ShapeDtypeStruct((count, rows_y, rows_z, length), jnp.float32),
            jax.ShapeDtypeStruct((count, count), jnp.float32),
        ),
        in_specs=[whole, whole, whole],
        out_specs=(planes, pl.BlockSpec((count, count), lambda i: (0, 0))),
        compiler_params=pltpu.CompilerParams(vmem_limit_bytes=vmem_limit),
    )(basis, factor, splat)


def solution(mesh):
    placed = (
        P("py", "pz", None),
        P("py", "pz", None),
        P("py", "pz", None),
        P("py", "pz", None),
        P(),
    )
    return jax.shard_map(
        on_device,
        mesh=mesh,
        in_specs=placed,
        out_specs=(P(None, "py", "pz", None), P()),
        check_vma=False,
    )
```

```python
import functools
import math

import jax
import jax.numpy as jnp
from jax import lax
from jax.experimental import pallas as pl
from jax.experimental.pallas import tpu as pltpu
from jax.sharding import PartitionSpec as P

step_scale = 0.125
MESH = pl.DeviceIdType.MESH
LANES = 128
SUBLANES = 8
WAYS = ((1, 0), (-1, 0), (0, 1), (0, -1), (1, 1), (1, -1), (-1, 1), (-1, -1))


def two_sum(a, b):
    total = a + b
    virtual = total - a
    return total, (a - (total - virtual)) + (b - virtual)


def split(a):
    scaled = a * 4097.0
    high = scaled - (scaled - a)
    return high, a - high


def two_product(a, b):
    product = a * b
    a_high, a_low = split(a)
    b_high, b_low = split(b)
    error = ((a_high * b_high - product) + a_high * b_low + a_low * b_high) + a_low * b_low
    return product, error


def pair_add(a, b):
    total, error = two_sum(a[0], b[0])
    return total, error + (a[1] + b[1])


def renormal(a):
    total = a[0] + a[1]
    return total, a[1] - (total - a[0])


def tree(parts):
    while len(parts) > 1:
        rest = parts[len(parts) // 2 * 2 :]
        parts = [pair_add(parts[i], parts[i + 1]) for i in range(0, len(parts) - 1, 2)] + rest
    return parts[0]


AT_Z, AT_X, AT_Y, AT_BEHIND = range(4)


def sum_pairs(parts):
    while len(parts) > 1:
        rest = parts[len(parts) // 2 * 2 :]
        added = []
        for i in range(0, len(parts) - 1, 2):
            total, error = two_sum(parts[i][0], parts[i + 1][0])
            added.append((total, error + (parts[i][1] + parts[i + 1][1])))
        parts = added + rest
    return parts[0]


def sum_rows(tiles):
    zero = jnp.zeros_like(tiles[0])
    total = sum_pairs([(tile, zero) for tile in tiles])
    shift = SUBLANES // 2
    while shift:
        total = pair_add(total, tuple(pltpu.roll(piece, shift, 0) for piece in total))
        shift //= 2
    return total


def fold(total):
    lead, minor = total
    return renormal((lead, minor + pltpu.roll(lead + minor, LANES // 2, 1)))


def wrap(high, low):
    lane = lax.broadcasted_iota(jnp.int32, high.shape, 1)
    return jnp.where(lane < LANES // 2, high, pltpu.roll(low, LANES // 2, 1))


def plan(depth):
    first = depth % 3 or 3
    return (first,) + (3,) * ((depth - first) // 3)


def stages_of(count_y, count_z):
    if count_y * count_z <= 64:
        return (("py", "pz"),)
    return (("pz",), ("py",))


def radii_of(count_y, count_z):
    radii = [1]
    while 2 * radii[-1] < max(count_y, count_z) - 1:
        radii.append(2 * radii[-1])
    return tuple(radii)


def first_pair(column):
    return column * (column + 1) // 2


def kernel(
    groups,
    count_y,
    count_z,
    root_cells,
    start_hbm,
    x_hbm,
    y_hbm,
    z_hbm,
    shifts_hbm,
    field,
    triangle,
    splat,
    coef,
    coef_late,
    partial,
    row_source,
    known,
    shifts,
    *rest,
):
    stages = stages_of(count_y, count_z)
    row_buffers = rest[: len(stages)]
    load_sem, send_sem, recv_sem, coef_send, coef_recv, row_send, row_recv = rest[len(stages) :]
    depth = shifts.shape[0]
    count = depth + 1
    rows_y, rows_z, length = start_hbm.shape
    span_y, span_z = field.shape[1:3]
    half_y, half_z = (span_y - rows_y) // 2, (span_z - rows_z) // 2
    padded = triangle.shape[0]
    sizes = {"py": count_y, "pz": count_z}
    me = {"py": lax.axis_index("py"), "pz": lax.axis_index("pz")}
    me_y, me_z = me["py"], me["pz"]
    most = max(groups)

    has = []
    comes = []
    target = []
    for dy, dz in WAYS:
        ahead, behind = [], []
        for step, at, size in ((dy, me_y, count_y), (dz, me_z, count_z)):
            if step:
                up, down = at < size - 1, at > 0
                ahead.append(up if step > 0 else down)
                behind.append(down if step > 0 else up)
        has.append(functools.reduce(jnp.logical_and, ahead))
        comes.append(functools.reduce(jnp.logical_and, behind))
        target.append({"py": me_y + dy, "pz": me_z + dz})

    own = (pl.ds(half_y, rows_y), pl.ds(0, rows_z))
    loads = [
        pltpu.make_async_copy(source, place.at[own], load_sem.at[i])
        for i, (source, place) in enumerate(
            (
                (start_hbm, field.at[0]),
                (z_hbm, coef.at[AT_Z]),
                (y_hbm, coef.at[AT_Y]),
                (x_hbm, coef.at[AT_X]),
            )
        )
    ]
    loads.append(pltpu.make_async_copy(shifts_hbm, shifts, load_sem.at[4]))
    for load in loads:
        load.start()

    radii = radii_of(count_y, count_z) if len(stages) == 1 else ()

    def in_reach(radius):
        spans = [jnp.minimum(at + radius, size - 1) - jnp.maximum(at - radius, 0) + 1 for at, size in ((me_y, count_y), (me_z, count_z))]
        return spans[0] * spans[1] - 1

    def pass_on(step):
        radius = radii[step]

        def one(other, carry):
            other_y, other_z = lax.div(other, count_z), lax.rem(other, count_z)
            near = jnp.logical_and(jnp.abs(other_y - me_y) <= radius, jnp.abs(other_z - me_z) <= radius)
            near = jnp.logical_and(near, jnp.logical_or(other_y != me_y, other_z != me_z))
            pl.when(near)(
                lambda: pl.semaphore_signal(
                    known.at[step], inc=1, device_id={"py": other_y, "pz": other_z}, device_id_type=MESH
                )
            )
            return carry

        lax.fori_loop(0, count_y * count_z, one, 0)

    def heard(step):
        pl.semaphore_wait(known.at[step], in_reach(radii[step]))

    barrier = pltpu.get_barrier_semaphore()
    if radii:
        expected = in_reach(1)
        for way in range(8):
            pl.when(has[way])(
                lambda way=way: pl.semaphore_signal(
                    barrier, inc=1, device_id=target[way], device_id_type=MESH
                )
            )
    else:
        expected = count_y + count_z - 2
        for axis, size in sizes.items():
            def greet(away, carry):
                pl.semaphore_signal(
                    barrier, inc=1, device_id={axis: lax.rem(me[axis] + away, size)}, device_id_type=MESH
                )
                return carry

            lax.fori_loop(1, size, greet, 0)
        for way in range(4, 8):
            pl.when(has[way])(
                lambda way=way: pl.semaphore_signal(
                    barrier, inc=1, device_id=target[way], device_id_type=MESH
                )
            )
            expected = expected + jnp.where(comes[way], 1, 0)

    def ends_y(step, first, last):
        if step > 0:
            return pl.ds(half_y + rows_y - last, last - first), pl.ds(half_y - last, last - first)
        if step < 0:
            return pl.ds(half_y + first, last - first), pl.ds(half_y + rows_y + first, last - first)
        return pl.ds(half_y, rows_y), pl.ds(half_y, rows_y)

    def ends_z(step, first, last):
        if step > 0:
            return pl.ds(rows_z - last, last - first), pl.ds(span_z - last, last - first)
        if step < 0:
            return pl.ds(first, last - first), pl.ds(rows_z + first, last - first)
        return pl.ds(0, rows_z), pl.ds(0, rows_z)

    def copy(array, which, way, y_band, z_band, sends, recvs, index, place=None):
        dy, dz = WAYS[way]
        from_y, to_y = ends_y(dy, *y_band)
        from_z, to_z = ends_z(dz, *z_band)
        return way, pltpu.make_async_remote_copy(
            src_ref=array.at[which, from_y, from_z],
            dst_ref=(array if place is None else place).at[which, to_y, to_z],
            send_sem=sends.at[index],
            recv_sem=recvs.at[index],
            device_id=target[way],
            device_id_type=MESH,
        )

    def start_all(copies):
        for way, each in copies:
            pl.when(has[way])(lambda each=each: each.start())

    def arrive_all(copies):
        for way, each in copies:
            pl.when(comes[way])(lambda each=each: each.wait_recv())

    def leave_all(copies):
        for way, each in copies:
            pl.when(has[way])(lambda each=each: each.wait_send())

    def field_copies(group):
        slot, reach = sum(groups[:group]), groups[group]
        bands = [(0, reach if way < 4 else reach - 1) for way in range(8 if reach > 1 else 4)]
        return [
            copy(field, slot, way, band, band, send_sem, recv_sem, group * 8 + way)
            for way, band in enumerate(bands)
        ]

    coef_parts = []

    def coef_band(before, after):
        copies = []

        def add(which, way, y_band, z_band, place=None):
            if y_band[1] > y_band[0] and z_band[1] > z_band[0]:
                index = len(coef_parts)
                coef_parts.append(index)
                copies.append(copy(coef, which, way, y_band, z_band, coef_send, coef_recv, index, place))

        for way, (dy, dz) in enumerate(WAYS):
            if way < 2:
                low = (max(before - 1, 0), after - 1)
                if dy < 0:
                    add(pl.ds(0, 3), way, low, low)
                else:
                    add(AT_Y, way, (before, after), (0, 1))
                    add(pl.ds(AT_Z, 2), way, low, (0, 1))
                continue
            place = coef_late if before else coef
            if way < 4:
                low = (0, after - 1)
                if dz < 0:
                    add(pl.ds(0, 3), way, low, low, place)
                else:
                    add(AT_Z, way, (0, 1), (0, after), place)
                    add(pl.ds(AT_X, 2), way, (0, 1), low, place)
            else:
                band = (0, max(after - (2 if dy < 0 and dz < 0 else 1), 0))
                add(pl.ds(0, 3), way, band, band, place)
        return copies

    fields = [field_copies(group) for group in range(len(groups))]
    early, late = coef_band(0, groups[0]), coef_band(groups[0], most) if most > groups[0] else []

    for load in loads:
        load.wait()
    pl.semaphore_wait(barrier, expected)
    start_all(fields[0])
    start_all(early)
    start_all(late)
    if radii:
        pass_on(0)

    def clear(block_y, block_z):
        shape = (block_y[1], block_z[1], length)
        where = (pl.ds(*block_y), pl.ds(*block_z))

        def one(piece, carry):
            coef[(piece, *where)] = jnp.zeros(shape, jnp.float32)
            coef_late[(piece, *where)] = jnp.zeros(shape, jnp.float32)
            return carry

        lax.fori_loop(0, 3, one, 0)
        for group in range(len(groups)):
            field[(sum(groups[:group]), *where)] = jnp.zeros(shape, jnp.float32)

    pl.when(me_y == 0)(lambda: clear((0, half_y), (0, span_z)))
    pl.when(me_y == count_y - 1)(lambda: clear((half_y + rows_y, half_y), (0, span_z)))
    pl.when(me_z == 0)(lambda: clear((0, span_y), (rows_z + half_z, half_z)))
    pl.when(me_z == count_z - 1)(lambda: clear((0, span_y), (rows_z, half_z)))

    pieces = range(length // LANES)
    last_piece = length // LANES - 1
    lane = lax.broadcasted_iota(jnp.int32, (rows_z, LANES), 1)
    sub = lax.broadcasted_iota(jnp.int32, (rows_z, LANES), 0)
    right_edge, left_edge = lane == LANES - 1, lane == 0
    top_row, bottom_row = sub == rows_z - 1, sub == 0
    inside_z = jnp.where(
        sub < half_z,
        jnp.where(me_z < count_z - 1, 1.0, 0.0),
        jnp.where(me_z > 0, 1.0, 0.0),
    )
    scale_below = jnp.where(me_y > 0, step_scale, 0.0)
    scale_above = jnp.where(me_y < count_y - 1, step_scale, 0.0)

    def shifted(rows):
        ahead = [pltpu.roll(row, LANES - 1, 1) for row in rows]
        behind = [pltpu.roll(row, 1, 1) for row in rows]
        return (
            [jnp.where(right_edge, ahead[x + 1] if x < last_piece else 0.0, ahead[x]) for x in pieces],
            [jnp.where(left_edge, behind[x - 1] if x else 0.0, behind[x]) for x in pieces],
        )

    def turn_x(array, first, last, tile):
        for y in range(first, last):
            where = [(y, pl.ds(tile * rows_z, rows_z), pl.ds(x * LANES, LANES)) for x in pieces]
            for at, behind in zip(where, shifted([array[(AT_X, *at)] for at in where])[1]):
                array[(AT_BEHIND, *at)] = behind

    def level(group, step):
        slot = sum(groups[:group]) + step
        left = groups[group] - step - 1
        shift = shifts[slot]
        tiles = (0, 1) if left else (0,)

        def at(tile, x):
            return pl.ds(tile * rows_z, rows_z), pl.ds(x * LANES, LANES)

        def value(y, tile, x):
            return field[(slot, y, *at(tile, x))]

        beyond = coef_late if group else coef

        def factor(which, y, tile, x):
            return (beyond if tile else coef)[(which, y, *at(tile, x))]

        def edge(array, which, y, z, x):
            return array[which, y, pl.ds(z, 1), pl.ds(x * LANES, LANES)]

        def part_z(y, x, outer):
            if outer:
                rows = [value(y, tile, x) for tile in tiles]
                turned = [pltpu.roll(row, rows_z - 1, 0) for row in rows]
                flux = [
                    factor(AT_Z, y, tile, x)
                    * (rows[tile] - jnp.where(top_row, turned[1 - tile], turned[tile]))
                    for tile in tiles
                ]
                turned = [pltpu.roll(each, 1, 0) for each in flux]
                return [
                    flux[tile] - jnp.where(bottom_row, turned[1 - tile], turned[tile]) for tile in tiles
                ]
            row = value(y, 0, x)
            up = jnp.where(top_row, edge(field, slot, y, rows_z, x), pltpu.roll(row, rows_z - 1, 0))
            flux = factor(AT_Z, y, 0, x) * (row - up)
            below = edge(beyond, AT_Z, y, span_z - 1, x) * (edge(field, slot, y, span_z - 1, x) - row[0:1, :])
            return [flux - jnp.where(bottom_row, below, pltpu.roll(flux, 1, 0))]

        def part_x(y, tile):
            rows = [value(y, tile, x) for x in pieces]
            ahead, behind = shifted(rows)
            return [
                factor(AT_X, y, tile, x) * (rows[x] - ahead[x])
                + factor(AT_BEHIND, y, tile, x) * (rows[x] - behind[x])
                for x in pieces
            ]

        def flux_y(y, tile, x):
            return factor(AT_Y, y, tile, x) * (value(y, tile, x) - value(y + 1, tile, x))

        first, last = half_y - left, half_y + rows_y + left

        carried = {}
        for y in range(first, last):
            scale = step_scale if half_y <= y < half_y + rows_y else scale_below if y < half_y else scale_above
            here = tiles[:1] if left and y in (first, last - 1) else tiles
            along_x = [part_x(y, tile) for tile in here]
            along_z = [part_z(y, x, len(here) > 1) for x in pieces]
            for tile in here:
                scale_tile = scale * inside_z if tile else scale
                for x in pieces:
                    flux = flux_y(y, tile, x)
                    below = carried[tile, x] if (tile, x) in carried else flux_y(y - 1, tile, x)
                    change = (flux - below) - shift * value(y, tile, x)
                    fresh = (along_x[tile][x] + along_z[x][tile]) + change
                    field[(slot + 1, y, *at(tile, x))] = fresh * scale_tile
                    carried[tile, x] = flux

    def gram(columns):
        pairs = [(i, j) for j in columns for i in range(j + 1)]

        def plane(y, totals):
            totals = list(totals)
            for x in range(0, length, LANES):
                pieces = [field[i, half_y + y, pl.ds(0, rows_z), pl.ds(x, LANES)] for i in range(max(columns) + 1)]
                for p, (i, j) in enumerate(pairs):
                    totals[p] = totals[p] + pieces[i] * pieces[j]
            return tuple(totals)

        zero = jnp.zeros((SUBLANES, LANES), jnp.float32)
        totals = lax.fori_loop(0, rows_y, plane, (zero,) * len(pairs))
        for (i, j), total in zip(pairs, totals):
            partial[pl.ds((first_pair(j) + i) * SUBLANES, SUBLANES), :] = total

    pairs = first_pair(count)
    many = partial.shape[0] // SUBLANES
    for at in range(pairs, many):
        partial[pl.ds(at * SUBLANES, SUBLANES), :] = jnp.zeros((SUBLANES, LANES), jnp.float32)

    turn_x(coef, half_y, half_y + rows_y, 0)
    for group, applications in enumerate(groups):
        if group:
            start_all(fields[group])
        if group == 1:
            arrive_all(late)
            turn_x(coef, half_y - most + 1, half_y - groups[0] + 1, 0)
            turn_x(coef, half_y + rows_y + groups[0] - 1, half_y + rows_y + most - 1, 0)
            turn_x(coef_late, half_y - most + 2, half_y + rows_y + most - 2, 1)
        if group:
            gram(range(0 if group == 1 else sum(groups[: group - 1]) + 1, sum(groups[:group]) + 1))
        arrive_all(fields[group])
        if group < len(radii) - 1:
            heard(group)
        if group + 1 < len(radii):
            pass_on(group + 1)
        if group == 0:
            arrive_all(early)
        if group == 0:
            reach = applications - 1
            turn_x(coef, half_y - reach, half_y, 0)
            turn_x(coef, half_y + rows_y, half_y + rows_y + reach, 0)
            turn_x(coef, half_y - reach + 1, half_y + rows_y + reach - 1, 1)
        for step in range(applications):
            level(group, step)
    gram(range(sum(groups[:-1]) + 1, count))

    high, low = sum_pairs(
        [
            (partial[pl.ds(s, many, stride=SUBLANES), :], jnp.zeros((many, LANES), jnp.float32))
            for s in range(SUBLANES)
        ]
    )
    fill = jnp.zeros((LANES // 2 - many, LANES), jnp.float32)
    turned = jnp.concatenate([high, fill, low, fill], axis=0).T
    total = fold(sum_rows([turned[y : y + SUBLANES] for y in range(0, LANES, SUBLANES)]))
    if radii:
        heard(len(radii) - 1)
    sent = []
    for stage, axes in enumerate(stages):
        buffer = row_buffers[stage]
        size = math.prod(sizes[axis] for axis in axes)
        index = functools.reduce(lambda at, axis: at * sizes[axis] + me[axis], axes, 0)
        row_source[stage] = wrap(*total)
        if buffer.shape[0] > size:
            buffer[pl.ds(size, buffer.shape[0] - size), :] = jnp.zeros(
                (buffer.shape[0] - size, LANES), jnp.float32
            )

        def send(away, carry):
            other = lax.rem(index + away, size)
            device = {}
            for axis in reversed(axes):
                device[axis] = lax.rem(other, sizes[axis])
                other = lax.div(other, sizes[axis])
            pltpu.make_async_remote_copy(
                src_ref=row_source.at[stage, pl.ds(0, 1)],
                dst_ref=buffer.at[pl.ds(index, 1)],
                send_sem=row_send.at[stage],
                recv_sem=row_recv.at[stage],
                device_id=device,
                device_id_type=MESH,
            ).start()
            return carry

        lax.fori_loop(1, size, send, 0)
        buffer[pl.ds(index, 1), :] = row_source[stage, pl.ds(0, 1), :]
        if stage == 0:
            for copies in (*fields, early, late):
                leave_all(copies)
        others = buffer.at[pl.ds(0, size - 1)]
        pltpu.make_async_copy(others, others, row_recv.at[stage]).wait()
        sent.append(pltpu.make_async_copy(others, others, row_send.at[stage]))
        rows = [buffer[pl.ds(y, SUBLANES), :] for y in range(0, buffer.shape[0], SUBLANES)]
        total = fold(sum_rows(rows))

    high, low = {}, {}
    for j in range(count):
        for i in range(j + 1):
            p = first_pair(j) + i
            high[i, j], low[i, j] = (
                jnp.broadcast_to(piece[:, p : p + 1], (SUBLANES, LANES)) for piece in total
            )
    square_sub = lax.broadcasted_iota(jnp.int32, (padded, LANES), 0)
    square_lane = lax.broadcasted_iota(jnp.int32, (padded, LANES), 1)
    tri = jnp.zeros((padded, LANES), jnp.float32)
    for k in range(count):
        for j in range(k, count):
            high[k, j], low[k, j] = renormal((high[k, j], low[k, j]))
        d_high, d_low = high[k, k], low[k, k]
        root = jnp.sqrt(d_high)
        for j in range(k, count):
            value = high[k, j] / root / root_cells
            splat[k * count + j] = 1.0 / value if j == k else value
            here = jnp.logical_and(square_sub == k, square_lane == j)
            tri = jnp.where(here, jnp.concatenate([value] * (padded // SUBLANES), axis=0), tri)
        inverse = 1.0 / d_high
        halves = {j: split(high[k, j]) for j in range(k, count)}
        for i in range(k + 1, count):
            lead = high[k, i] * inverse
            lead_high, lead_low = split(lead)

            def times(j):
                product = lead * high[k, j]
                big, small = halves[j]
                error = ((lead_high * big - product) + lead_high * small + lead_low * big) + lead_low * small
                return product, error

            product, error = times(k)
            minor = (((high[k, i] - product) - error) + (low[k, i] - lead * d_low)) * inverse
            for j in range(i, count):
                product, error = times(j)
                error = error + (high[k, j] * minor + low[k, j] * lead)
                rest_high, rest_low = two_sum(high[i, j], -product)
                high[i, j], low[i, j] = rest_high, rest_low + (low[i, j] - error)
    triangle[...] = tri
    for each in sent:
        each.wait()


def substitute(basis, factor, splat, out, triangle, solved_rows, sems):
    count, rows_y, rows_z, length = solved_rows.shape
    first = (basis.shape[1] - rows_y) // 2
    triangle[...] = factor[:count, :count]

    def plane(y, carry):
        for x in range(0, length, LANES):
            solved = []
            for i in range(count):
                value = basis[i, first + y, pl.ds(0, rows_z), x : x + LANES]
                for k in range(i):
                    value = value - splat[k * count + i] * solved[k]
                value = value * splat[i * count + i]
                solved_rows[i, y, :, x : x + LANES] = value
                solved.append(value)
        return carry

    copies = []
    part = rows_y // 4
    for p in range(4):
        lax.fori_loop(p * part, (p + 1) * part, plane, 0, unroll=2)
        rows = pl.ds(p * part, part)
        copies.append(pltpu.make_async_copy(solved_rows.at[:, rows], out.at[:, rows], sems.at[p]))
        copies[-1].start()
    for each in copies:
        each.wait()


def on_device(start, coef_x, coef_y, coef_z, shifts):
    rows_y, rows_z, length = start.shape
    depth = shifts.shape[0]
    count = depth + 1
    padded = (count + SUBLANES - 1) // SUBLANES * SUBLANES
    count_y, count_z = lax.axis_size("py"), lax.axis_size("pz")
    cells = length * rows_y * rows_z * count_y * count_z
    groups = plan(depth)
    span_y, span_z = rows_y + 8, rows_z + 8
    stages = stages_of(count_y, count_z)
    sizes = {"py": count_y, "pz": count_z}
    members = [math.prod(sizes[axis] for axis in axes) for axes in stages]
    whole = pl.BlockSpec(memory_space=pltpu.VMEM)
    many = (first_pair(count) + SUBLANES - 1) // SUBLANES * SUBLANES
    pltpu_f32 = lambda *shape: pltpu.VMEM(shape, jnp.float32)
    dma = pltpu.SemaphoreType.DMA
    vmem_limit = 2**26 - 4 * (count * span_y * span_z * length) - 2**19
    anywhere = pl.BlockSpec(memory_space=pl.ANY)
    basis, factor, splat = pl.pallas_call(
        functools.partial(kernel, groups, count_y, count_z, math.sqrt(cells)),
        out_shape=(
            pltpu_f32(count, span_y, span_z, length),
            pltpu_f32(padded, LANES),
            pltpu_f32(count * count, SUBLANES, LANES),
        ),
        in_specs=[anywhere] * 5,
        out_specs=(whole, whole, whole),
        scratch_shapes=[
            pltpu_f32(4, span_y, span_z, length),
            pltpu_f32(4, span_y, span_z, length),
            pltpu_f32(many * SUBLANES, LANES),
            pltpu_f32(len(stages), SUBLANES, LANES),
            pltpu.SemaphoreType.REGULAR((8,)),
            pltpu.SMEM((depth,), jnp.float32),
            *[pltpu_f32((n + SUBLANES - 1) // SUBLANES * SUBLANES, LANES) for n in members],
            dma((5,)),
            dma((len(groups) * 8,)),
            dma((len(groups) * 8,)),
            dma((32,)),
            dma((32,)),
            dma((len(stages),)),
            dma((len(stages),)),
        ],
        compiler_params=pltpu.CompilerParams(
            collective_id=0, has_side_effects=True, vmem_limit_bytes=vmem_limit
        ),
    )(start, coef_x, coef_y, coef_z, shifts)
    basis = pltpu.with_memory_space_constraint(basis, pltpu.VMEM)
    factor = pltpu.with_memory_space_constraint(factor, pltpu.VMEM)
    splat = pltpu.with_memory_space_constraint(splat, pltpu.VMEM)
    return pl.pallas_call(
        substitute,
        out_shape=(
            jax.ShapeDtypeStruct((count, rows_y, rows_z, length), jnp.float32),
            jax.ShapeDtypeStruct((count, count), jnp.float32),
        ),
        in_specs=[whole, whole, whole],
        out_specs=(anywhere, whole),
        scratch_shapes=[pltpu_f32(count, rows_y, rows_z, length), dma((4,))],
        compiler_params=pltpu.CompilerParams(vmem_limit_bytes=vmem_limit),
    )(basis, factor, splat)


def solution(mesh):
    placed = (
        P("py", "pz", None),
        P("py", "pz", None),
        P("py", "pz", None),
        P("py", "pz", None),
        P(),
    )
    return jax.shard_map(
        on_device,
        mesh=mesh,
        in_specs=placed,
        out_specs=(P(None, "py", "pz", None), P()),
        check_vma=False,
    )
```

```python
import functools
import math

import jax
import jax.numpy as jnp
from jax import lax
from jax.experimental import pallas as pl
from jax.experimental.pallas import tpu as pltpu
from jax.sharding import PartitionSpec as P

step_scale = 0.125
MESH = pl.DeviceIdType.MESH
LANES = 128
SUBLANES = 8
WAYS = ((1, 0), (-1, 0), (0, 1), (0, -1), (1, 1), (1, -1), (-1, 1), (-1, -1))


def two_sum(a, b):
    total = a + b
    virtual = total - a
    return total, (a - (total - virtual)) + (b - virtual)


def split(a):
    scaled = a * 4097.0
    high = scaled - (scaled - a)
    return high, a - high


def two_product(a, b):
    product = a * b
    a_high, a_low = split(a)
    b_high, b_low = split(b)
    error = ((a_high * b_high - product) + a_high * b_low + a_low * b_high) + a_low * b_low
    return product, error


def pair_add(a, b):
    total, error = two_sum(a[0], b[0])
    return total, error + (a[1] + b[1])


def renormal(a):
    total = a[0] + a[1]
    return total, a[1] - (total - a[0])


def tree(parts):
    while len(parts) > 1:
        rest = parts[len(parts) // 2 * 2 :]
        parts = [pair_add(parts[i], parts[i + 1]) for i in range(0, len(parts) - 1, 2)] + rest
    return parts[0]


AT_Z, AT_X, AT_Y, AT_BEHIND = range(4)


def sum_pairs(parts):
    while len(parts) > 1:
        rest = parts[len(parts) // 2 * 2 :]
        added = []
        for i in range(0, len(parts) - 1, 2):
            total, error = two_sum(parts[i][0], parts[i + 1][0])
            added.append((total, error + (parts[i][1] + parts[i + 1][1])))
        parts = added + rest
    return parts[0]


def sum_rows(tiles):
    zero = jnp.zeros_like(tiles[0])
    total = sum_pairs([(tile, zero) for tile in tiles])
    shift = SUBLANES // 2
    while shift:
        total = pair_add(total, tuple(pltpu.roll(piece, shift, 0) for piece in total))
        shift //= 2
    return total


def fold(total):
    lead, minor = total
    return renormal((lead, minor + pltpu.roll(lead + minor, LANES // 2, 1)))


def packed(lead, minor):
    lane = lax.broadcasted_iota(jnp.int32, lead.shape, 1)
    return jnp.where(lane < LANES // 2, lead, (lead + minor) + pltpu.roll(minor, LANES // 2, 1))


def plan(depth):
    first = depth % 3 or 3
    return (first,) + (3,) * ((depth - first) // 3)


def stages_of(count_y, count_z):
    if count_y * count_z <= 64:
        return (("py", "pz"),)
    return (("pz",), ("py",))


def radii_of(count_y, count_z):
    radii = [1]
    while 2 * radii[-1] < max(count_y, count_z) - 1:
        radii.append(2 * radii[-1])
    return tuple(radii)


def first_pair(column):
    return column * (column + 1) // 2


def kernel(
    groups,
    count_y,
    count_z,
    root_cells,
    start_hbm,
    x_hbm,
    y_hbm,
    z_hbm,
    shifts_hbm,
    field,
    triangle,
    splat,
    coef,
    coef_late,
    partial,
    row_source,
    known,
    shifts,
    *rest,
):
    stages = stages_of(count_y, count_z)
    row_buffers = rest[: len(stages)]
    load_sem, send_sem, recv_sem, coef_send, coef_recv, row_send, row_recv = rest[len(stages) :]
    depth = shifts.shape[0]
    count = depth + 1
    rows_y, rows_z, length = start_hbm.shape
    span_y, span_z = field.shape[1:3]
    half_y, half_z = (span_y - rows_y) // 2, (span_z - rows_z) // 2
    padded = triangle.shape[0]
    sizes = {"py": count_y, "pz": count_z}
    me = {"py": lax.axis_index("py"), "pz": lax.axis_index("pz")}
    me_y, me_z = me["py"], me["pz"]
    most = max(groups)

    has = []
    comes = []
    target = []
    for dy, dz in WAYS:
        ahead, behind = [], []
        for step, at, size in ((dy, me_y, count_y), (dz, me_z, count_z)):
            if step:
                up, down = at < size - 1, at > 0
                ahead.append(up if step > 0 else down)
                behind.append(down if step > 0 else up)
        has.append(functools.reduce(jnp.logical_and, ahead))
        comes.append(functools.reduce(jnp.logical_and, behind))
        target.append({"py": me_y + dy, "pz": me_z + dz})

    own = (pl.ds(half_y, rows_y), pl.ds(0, rows_z))
    loads = [
        pltpu.make_async_copy(source, place.at[own], load_sem.at[i])
        for i, (source, place) in enumerate(
            (
                (start_hbm, field.at[0]),
                (z_hbm, coef.at[AT_Z]),
                (y_hbm, coef.at[AT_Y]),
                (x_hbm, coef.at[AT_X]),
            )
        )
    ]
    loads.append(pltpu.make_async_copy(shifts_hbm, shifts, load_sem.at[4]))
    for load in loads:
        load.start()

    radii = radii_of(count_y, count_z) if len(stages) == 1 else ()

    def in_reach(radius):
        spans = [jnp.minimum(at + radius, size - 1) - jnp.maximum(at - radius, 0) + 1 for at, size in ((me_y, count_y), (me_z, count_z))]
        return spans[0] * spans[1] - 1

    def pass_on(step):
        radius = radii[step]

        def one(other, carry):
            other_y, other_z = lax.div(other, count_z), lax.rem(other, count_z)
            near = jnp.logical_and(jnp.abs(other_y - me_y) <= radius, jnp.abs(other_z - me_z) <= radius)
            near = jnp.logical_and(near, jnp.logical_or(other_y != me_y, other_z != me_z))
            pl.when(near)(
                lambda: pl.semaphore_signal(
                    known.at[step], inc=1, device_id={"py": other_y, "pz": other_z}, device_id_type=MESH
                )
            )
            return carry

        lax.fori_loop(0, count_y * count_z, one, 0)

    def heard(step):
        pl.semaphore_wait(known.at[step], in_reach(radii[step]))

    barrier = pltpu.get_barrier_semaphore()
    if radii:
        expected = in_reach(1)
        for way in range(8):
            pl.when(has[way])(
                lambda way=way: pl.semaphore_signal(
                    barrier, inc=1, device_id=target[way], device_id_type=MESH
                )
            )
    else:
        expected = count_y + count_z - 2
        for axis, size in sizes.items():
            def greet(away, carry):
                pl.semaphore_signal(
                    barrier, inc=1, device_id={axis: lax.rem(me[axis] + away, size)}, device_id_type=MESH
                )
                return carry

            lax.fori_loop(1, size, greet, 0)
        for way in range(4, 8):
            pl.when(has[way])(
                lambda way=way: pl.semaphore_signal(
                    barrier, inc=1, device_id=target[way], device_id_type=MESH
                )
            )
            expected = expected + jnp.where(comes[way], 1, 0)

    def ends_y(step, first, last):
        if step > 0:
            return pl.ds(half_y + rows_y - last, last - first), pl.ds(half_y - last, last - first)
        if step < 0:
            return pl.ds(half_y + first, last - first), pl.ds(half_y + rows_y + first, last - first)
        return pl.ds(half_y, rows_y), pl.ds(half_y, rows_y)

    def ends_z(step, first, last):
        if step > 0:
            return pl.ds(rows_z - last, last - first), pl.ds(span_z - last, last - first)
        if step < 0:
            return pl.ds(first, last - first), pl.ds(rows_z + first, last - first)
        return pl.ds(0, rows_z), pl.ds(0, rows_z)

    def copy(array, which, way, y_band, z_band, sends, recvs, index, place=None):
        dy, dz = WAYS[way]
        from_y, to_y = ends_y(dy, *y_band)
        from_z, to_z = ends_z(dz, *z_band)
        return way, pltpu.make_async_remote_copy(
            src_ref=array.at[which, from_y, from_z],
            dst_ref=(array if place is None else place).at[which, to_y, to_z],
            send_sem=sends.at[index],
            recv_sem=recvs.at[index],
            device_id=target[way],
            device_id_type=MESH,
        )

    def start_all(copies):
        for way, each in copies:
            pl.when(has[way])(lambda each=each: each.start())

    def arrive_all(copies):
        for way, each in copies:
            pl.when(comes[way])(lambda each=each: each.wait_recv())

    def leave_all(copies):
        for way, each in copies:
            pl.when(has[way])(lambda each=each: each.wait_send())

    def field_copies(group):
        slot, reach = sum(groups[:group]), groups[group]
        bands = [(0, reach if way < 4 else reach - 1) for way in range(8 if reach > 1 else 4)]
        return [
            copy(field, slot, way, band, band, send_sem, recv_sem, group * 8 + way)
            for way, band in enumerate(bands)
        ]

    coef_parts = []

    def coef_band(before, after):
        copies = []

        def add(which, way, y_band, z_band, place=None):
            if y_band[1] > y_band[0] and z_band[1] > z_band[0]:
                index = len(coef_parts)
                coef_parts.append(index)
                copies.append(copy(coef, which, way, y_band, z_band, coef_send, coef_recv, index, place))

        for way, (dy, dz) in enumerate(WAYS):
            if way < 2:
                low = (max(before - 1, 0), after - 1)
                if dy < 0:
                    add(pl.ds(0, 3), way, low, low)
                else:
                    add(AT_Y, way, (before, after), (0, 1))
                    add(pl.ds(AT_Z, 2), way, low, (0, 1))
                continue
            place = coef_late if before else coef
            if way < 4:
                low = (0, after - 1)
                if dz < 0:
                    add(pl.ds(0, 3), way, low, low, place)
                else:
                    add(AT_Z, way, (0, 1), (0, after), place)
                    add(pl.ds(AT_X, 2), way, (0, 1), low, place)
            else:
                band = (0, max(after - (2 if dy < 0 and dz < 0 else 1), 0))
                add(pl.ds(0, 3), way, band, band, place)
        return copies

    fields = [field_copies(group) for group in range(len(groups))]
    early, late = coef_band(0, groups[0]), coef_band(groups[0], most) if most > groups[0] else []

    for load in loads:
        load.wait()
    pl.semaphore_wait(barrier, expected)
    start_all(fields[0])
    start_all(early)
    start_all(late)
    if radii:
        pass_on(0)

    def clear(block_y, block_z):
        shape = (block_y[1], block_z[1], length)
        where = (pl.ds(*block_y), pl.ds(*block_z))

        def one(piece, carry):
            coef[(piece, *where)] = jnp.zeros(shape, jnp.float32)
            coef_late[(piece, *where)] = jnp.zeros(shape, jnp.float32)
            return carry

        lax.fori_loop(0, 3, one, 0)
        for group in range(len(groups)):
            field[(sum(groups[:group]), *where)] = jnp.zeros(shape, jnp.float32)

    pl.when(me_y == 0)(lambda: clear((0, half_y), (0, span_z)))
    pl.when(me_y == count_y - 1)(lambda: clear((half_y + rows_y, half_y), (0, span_z)))
    pl.when(me_z == 0)(lambda: clear((0, span_y), (rows_z + half_z, half_z)))
    pl.when(me_z == count_z - 1)(lambda: clear((0, span_y), (rows_z, half_z)))

    pieces = range(length // LANES)
    last_piece = length // LANES - 1
    lane = lax.broadcasted_iota(jnp.int32, (rows_z, LANES), 1)
    sub = lax.broadcasted_iota(jnp.int32, (rows_z, LANES), 0)
    right_edge, left_edge = lane == LANES - 1, lane == 0
    top_row, bottom_row = sub == rows_z - 1, sub == 0
    inside_z = jnp.where(
        sub < half_z,
        jnp.where(me_z < count_z - 1, 1.0, 0.0),
        jnp.where(me_z > 0, 1.0, 0.0),
    )
    scale_below = jnp.where(me_y > 0, step_scale, 0.0)
    scale_above = jnp.where(me_y < count_y - 1, step_scale, 0.0)

    def shifted(rows):
        ahead = [pltpu.roll(row, LANES - 1, 1) for row in rows]
        behind = [pltpu.roll(row, 1, 1) for row in rows]
        return (
            [jnp.where(right_edge, ahead[x + 1] if x < last_piece else 0.0, ahead[x]) for x in pieces],
            [jnp.where(left_edge, behind[x - 1] if x else 0.0, behind[x]) for x in pieces],
        )

    def turn_x(array, first, last, tile):
        for y in range(first, last):
            where = [(y, pl.ds(tile * rows_z, rows_z), pl.ds(x * LANES, LANES)) for x in pieces]
            for at, behind in zip(where, shifted([array[(AT_X, *at)] for at in where])[1]):
                array[(AT_BEHIND, *at)] = behind

    def level(group, step):
        slot = sum(groups[:group]) + step
        left = groups[group] - step - 1
        shift = shifts[slot]
        tiles = (0, 1) if left else (0,)

        def at(tile, x):
            return pl.ds(tile * rows_z, rows_z), pl.ds(x * LANES, LANES)

        def value(y, tile, x):
            return field[(slot, y, *at(tile, x))]

        beyond = coef_late if group else coef

        def factor(which, y, tile, x):
            return (beyond if tile else coef)[(which, y, *at(tile, x))]

        def edge(array, which, y, z, x):
            return array[which, y, pl.ds(z, 1), pl.ds(x * LANES, LANES)]

        def part_z(y, x, outer):
            if outer:
                rows = [value(y, tile, x) for tile in tiles]
                turned = [pltpu.roll(row, rows_z - 1, 0) for row in rows]
                flux = [
                    factor(AT_Z, y, tile, x)
                    * (rows[tile] - jnp.where(top_row, turned[1 - tile], turned[tile]))
                    for tile in tiles
                ]
                turned = [pltpu.roll(each, 1, 0) for each in flux]
                return [
                    flux[tile] - jnp.where(bottom_row, turned[1 - tile], turned[tile]) for tile in tiles
                ]
            row = value(y, 0, x)
            up = jnp.where(top_row, edge(field, slot, y, rows_z, x), pltpu.roll(row, rows_z - 1, 0))
            flux = factor(AT_Z, y, 0, x) * (row - up)
            below = edge(beyond, AT_Z, y, span_z - 1, x) * (edge(field, slot, y, span_z - 1, x) - row[0:1, :])
            return [flux - jnp.where(bottom_row, below, pltpu.roll(flux, 1, 0))]

        def part_x(y, tile):
            rows = [value(y, tile, x) for x in pieces]
            ahead, behind = shifted(rows)
            return [
                factor(AT_X, y, tile, x) * (rows[x] - ahead[x])
                + factor(AT_BEHIND, y, tile, x) * (rows[x] - behind[x])
                for x in pieces
            ]

        def flux_y(y, tile, x):
            return factor(AT_Y, y, tile, x) * (value(y, tile, x) - value(y + 1, tile, x))

        first, last = half_y - left, half_y + rows_y + left

        carried = {}
        for y in range(first, last):
            scale = step_scale if half_y <= y < half_y + rows_y else scale_below if y < half_y else scale_above
            here = tiles[:1] if left and y in (first, last - 1) else tiles
            along_x = [part_x(y, tile) for tile in here]
            along_z = [part_z(y, x, len(here) > 1) for x in pieces]
            for tile in here:
                scale_tile = scale * inside_z if tile else scale
                for x in pieces:
                    flux = flux_y(y, tile, x)
                    below = carried[tile, x] if (tile, x) in carried else flux_y(y - 1, tile, x)
                    change = (flux - below) - shift * value(y, tile, x)
                    fresh = (along_x[tile][x] + along_z[x][tile]) + change
                    field[(slot + 1, y, *at(tile, x))] = fresh * scale_tile
                    carried[tile, x] = flux

    def gram(columns):
        pairs = [(i, j) for j in columns for i in range(j + 1)]

        def plane(y, totals):
            totals = list(totals)
            for x in range(0, length, LANES):
                pieces = [field[i, half_y + y, pl.ds(0, rows_z), pl.ds(x, LANES)] for i in range(max(columns) + 1)]
                for p, (i, j) in enumerate(pairs):
                    totals[p] = totals[p] + pieces[i] * pieces[j]
            return tuple(totals)

        zero = jnp.zeros((SUBLANES, LANES), jnp.float32)
        totals = lax.fori_loop(0, rows_y, plane, (zero,) * len(pairs))
        for (i, j), total in zip(pairs, totals):
            partial[pl.ds((first_pair(j) + i) * SUBLANES, SUBLANES), :] = total

    pairs = first_pair(count)
    many = partial.shape[0] // SUBLANES
    for at in range(pairs, many):
        partial[pl.ds(at * SUBLANES, SUBLANES), :] = jnp.zeros((SUBLANES, LANES), jnp.float32)

    turn_x(coef, half_y, half_y + rows_y, 0)
    for group, applications in enumerate(groups):
        if group:
            start_all(fields[group])
        if group == 1:
            arrive_all(late)
            turn_x(coef, half_y - most + 1, half_y - groups[0] + 1, 0)
            turn_x(coef, half_y + rows_y + groups[0] - 1, half_y + rows_y + most - 1, 0)
            turn_x(coef_late, half_y - most + 2, half_y + rows_y + most - 2, 1)
        if 0 < group < len(radii):
            heard(group - 1)
            pass_on(group)
        if group:
            gram(range(0 if group == 1 else sum(groups[: group - 1]) + 1, sum(groups[:group]) + 1))
        arrive_all(fields[group])
        if group == 0:
            arrive_all(early)
        if group == 0:
            reach = applications - 1
            turn_x(coef, half_y - reach, half_y, 0)
            turn_x(coef, half_y + rows_y, half_y + rows_y + reach, 0)
            turn_x(coef, half_y - reach + 1, half_y + rows_y + reach - 1, 1)
        for step in range(applications):
            level(group, step)
    gram(range(sum(groups[:-1]) + 1, count))

    high, low = sum_pairs(
        [
            (partial[pl.ds(s, many, stride=SUBLANES), :], jnp.zeros((many, LANES), jnp.float32))
            for s in range(SUBLANES)
        ]
    )
    fill = jnp.zeros((LANES // 2 - many, LANES), jnp.float32)
    turned = jnp.concatenate([high, fill, low, fill], axis=0).T
    total = sum_rows([turned[y : y + SUBLANES] for y in range(0, LANES, SUBLANES)])
    if radii:
        heard(len(radii) - 1)
    sent = []
    for stage, axes in enumerate(stages):
        buffer = row_buffers[stage]
        size = math.prod(sizes[axis] for axis in axes)
        index = functools.reduce(lambda at, axis: at * sizes[axis] + me[axis], axes, 0)
        row_source[stage] = packed(*total)
        if buffer.shape[0] > size:
            buffer[pl.ds(size, buffer.shape[0] - size), :] = jnp.zeros(
                (buffer.shape[0] - size, LANES), jnp.float32
            )

        def send(away, carry):
            other = lax.rem(index + away, size)
            device = {}
            for axis in reversed(axes):
                device[axis] = lax.rem(other, sizes[axis])
                other = lax.div(other, sizes[axis])
            pltpu.make_async_remote_copy(
                src_ref=row_source.at[stage, pl.ds(0, 1)],
                dst_ref=buffer.at[pl.ds(index, 1)],
                send_sem=row_send.at[stage],
                recv_sem=row_recv.at[stage],
                device_id=device,
                device_id_type=MESH,
            ).start()
            return carry

        lax.fori_loop(1, size, send, 0)
        buffer[pl.ds(index, 1), :] = row_source[stage, pl.ds(0, 1), :]
        if stage == 0:
            for copies in (*fields, early, late):
                leave_all(copies)
        others = buffer.at[pl.ds(0, size - 1)]
        pltpu.make_async_copy(others, others, row_recv.at[stage]).wait()
        sent.append(pltpu.make_async_copy(others, others, row_send.at[stage]))
        rows = [buffer[pl.ds(y, SUBLANES), :] for y in range(0, buffer.shape[0], SUBLANES)]
        total = sum_rows(rows)

    total = fold(total)
    high, low = {}, {}
    for j in range(count):
        for i in range(j + 1):
            p = first_pair(j) + i
            high[i, j], low[i, j] = (
                jnp.broadcast_to(piece[:, p : p + 1], (SUBLANES, LANES)) for piece in total
            )
    square_sub = lax.broadcasted_iota(jnp.int32, (padded, LANES), 0)
    square_lane = lax.broadcasted_iota(jnp.int32, (padded, LANES), 1)
    tri = jnp.zeros((padded, LANES), jnp.float32)
    for k in range(count):
        for j in range(k, count):
            high[k, j], low[k, j] = renormal((high[k, j], low[k, j]))
        d_high, d_low = high[k, k], low[k, k]
        root = jnp.sqrt(d_high)
        for j in range(k, count):
            value = high[k, j] / root / root_cells
            splat[k * count + j] = 1.0 / value if j == k else value
            here = jnp.logical_and(square_sub == k, square_lane == j)
            tri = jnp.where(here, jnp.concatenate([value] * (padded // SUBLANES), axis=0), tri)
        inverse = 1.0 / d_high
        halves = {j: split(high[k, j]) for j in range(k, count)}
        for i in range(k + 1, count):
            lead = high[k, i] * inverse
            lead_high, lead_low = split(lead)

            def times(j):
                product = lead * high[k, j]
                big, small = halves[j]
                error = ((lead_high * big - product) + lead_high * small + lead_low * big) + lead_low * small
                return product, error

            product, error = times(k)
            minor = (((high[k, i] - product) - error) + (low[k, i] - lead * d_low)) * inverse
            for j in range(i, count):
                product, error = times(j)
                error = error + (high[k, j] * minor + low[k, j] * lead)
                rest_high, rest_low = two_sum(high[i, j], -product)
                high[i, j], low[i, j] = rest_high, rest_low + (low[i, j] - error)
    triangle[...] = tri
    for each in sent:
        each.wait()


def substitute(basis, factor, splat, out, triangle, solved_rows, small, sems, small_sem):
    count, rows_y, rows_z, length = solved_rows.shape
    first = (basis.shape[1] - rows_y) // 2
    small[...] = factor[:count, :count]
    copies = [pltpu.make_async_copy(small, triangle, small_sem)]
    copies[0].start()

    def plane(y, carry):
        for x in range(0, length, LANES):
            solved = []
            for i in range(count):
                value = basis[i, first + y, pl.ds(0, rows_z), x : x + LANES]
                for k in range(i):
                    value = value - splat[k * count + i] * solved[k]
                value = value * splat[i * count + i]
                solved_rows[i, y, :, x : x + LANES] = value
                solved.append(value)
        return carry

    part = rows_y // 4
    for p in range(4):
        lax.fori_loop(p * part, (p + 1) * part, plane, 0, unroll=2)
        rows = pl.ds(p * part, part)
        copies.append(pltpu.make_async_copy(solved_rows.at[:, rows], out.at[:, rows], sems.at[p]))
        copies[-1].start()
    for each in copies:
        each.wait()


def on_device(start, coef_x, coef_y, coef_z, shifts):
    rows_y, rows_z, length = start.shape
    depth = shifts.shape[0]
    count = depth + 1
    padded = (count + SUBLANES - 1) // SUBLANES * SUBLANES
    count_y, count_z = lax.axis_size("py"), lax.axis_size("pz")
    cells = length * rows_y * rows_z * count_y * count_z
    groups = plan(depth)
    span_y, span_z = rows_y + 8, rows_z + 8
    stages = stages_of(count_y, count_z)
    sizes = {"py": count_y, "pz": count_z}
    members = [math.prod(sizes[axis] for axis in axes) for axes in stages]
    whole = pl.BlockSpec(memory_space=pltpu.VMEM)
    many = (first_pair(count) + SUBLANES - 1) // SUBLANES * SUBLANES
    pltpu_f32 = lambda *shape: pltpu.VMEM(shape, jnp.float32)
    dma = pltpu.SemaphoreType.DMA
    vmem_limit = 2**26 - 4 * (count * span_y * span_z * length) - 2**19
    anywhere = pl.BlockSpec(memory_space=pl.ANY)
    basis, factor, splat = pl.pallas_call(
        functools.partial(kernel, groups, count_y, count_z, math.sqrt(cells)),
        out_shape=(
            pltpu_f32(count, span_y, span_z, length),
            pltpu_f32(padded, LANES),
            pltpu_f32(count * count, SUBLANES, LANES),
        ),
        in_specs=[anywhere] * 5,
        out_specs=(whole, whole, whole),
        scratch_shapes=[
            pltpu_f32(4, span_y, span_z, length),
            pltpu_f32(4, span_y, span_z, length),
            pltpu_f32(many * SUBLANES, LANES),
            pltpu_f32(len(stages), SUBLANES, LANES),
            pltpu.SemaphoreType.REGULAR((8,)),
            pltpu.SMEM((depth,), jnp.float32),
            *[pltpu_f32((n + SUBLANES - 1) // SUBLANES * SUBLANES, LANES) for n in members],
            dma((5,)),
            dma((len(groups) * 8,)),
            dma((len(groups) * 8,)),
            dma((32,)),
            dma((32,)),
            dma((len(stages),)),
            dma((len(stages),)),
        ],
        compiler_params=pltpu.CompilerParams(
            collective_id=0, has_side_effects=True, vmem_limit_bytes=vmem_limit
        ),
    )(start, coef_x, coef_y, coef_z, shifts)
    basis = pltpu.with_memory_space_constraint(basis, pltpu.VMEM)
    factor = pltpu.with_memory_space_constraint(factor, pltpu.VMEM)
    splat = pltpu.with_memory_space_constraint(splat, pltpu.VMEM)
    return pl.pallas_call(
        substitute,
        out_shape=(
            jax.ShapeDtypeStruct((count, rows_y, rows_z, length), jnp.float32),
            jax.ShapeDtypeStruct((count, count), jnp.float32),
        ),
        in_specs=[whole, whole, whole],
        out_specs=(anywhere, anywhere),
        scratch_shapes=[pltpu_f32(count, rows_y, rows_z, length), pltpu_f32(count, count), dma((4,)), dma],
        compiler_params=pltpu.CompilerParams(vmem_limit_bytes=vmem_limit),
    )(basis, factor, splat)


def solution(mesh):
    placed = (
        P("py", "pz", None),
        P("py", "pz", None),
        P("py", "pz", None),
        P("py", "pz", None),
        P(),
    )
    return jax.shard_map(
        on_device,
        mesh=mesh,
        in_specs=placed,
        out_specs=(P(None, "py", "pz", None), P()),
        check_vma=False,
    )
```

```python
import functools
import math

import jax
import jax.numpy as jnp
from jax import lax
from jax.experimental import pallas as pl
from jax.experimental.pallas import tpu as pltpu
from jax.sharding import PartitionSpec as P

step_scale = 0.125
MESH = pl.DeviceIdType.MESH
LANES = 128
SUBLANES = 8
WAYS = ((1, 0), (-1, 0), (0, 1), (0, -1), (1, 1), (1, -1), (-1, 1), (-1, -1))


def two_sum(a, b):
    total = a + b
    virtual = total - a
    return total, (a - (total - virtual)) + (b - virtual)


def split(a):
    scaled = a * 4097.0
    high = scaled - (scaled - a)
    return high, a - high


def two_product(a, b):
    product = a * b
    a_high, a_low = split(a)
    b_high, b_low = split(b)
    error = ((a_high * b_high - product) + a_high * b_low + a_low * b_high) + a_low * b_low
    return product, error


def pair_add(a, b):
    total, error = two_sum(a[0], b[0])
    return total, error + (a[1] + b[1])


def renormal(a):
    total = a[0] + a[1]
    return total, a[1] - (total - a[0])


def tree(parts):
    while len(parts) > 1:
        rest = parts[len(parts) // 2 * 2 :]
        parts = [pair_add(parts[i], parts[i + 1]) for i in range(0, len(parts) - 1, 2)] + rest
    return parts[0]


AT_Z, AT_X, AT_Y, AT_BEHIND = range(4)


def sum_pairs(parts):
    while len(parts) > 1:
        rest = parts[len(parts) // 2 * 2 :]
        added = []
        for i in range(0, len(parts) - 1, 2):
            total, error = two_sum(parts[i][0], parts[i + 1][0])
            added.append((total, error + (parts[i][1] + parts[i + 1][1])))
        parts = added + rest
    return parts[0]


def sum_rows(tiles):
    zero = jnp.zeros_like(tiles[0])
    total = sum_pairs([(tile, zero) for tile in tiles])
    shift = SUBLANES // 2
    while shift:
        total = pair_add(total, tuple(pltpu.roll(piece, shift, 0) for piece in total))
        shift //= 2
    return total


def fold(total):
    lead, minor = total
    return renormal((lead, minor + pltpu.roll(lead + minor, LANES // 2, 1)))


def packed(lead, minor):
    lane = lax.broadcasted_iota(jnp.int32, lead.shape, 1)
    return jnp.where(lane < LANES // 2, lead, (lead + minor) + pltpu.roll(minor, LANES // 2, 1))


def plan(depth):
    first = depth % 3 or 3
    return (first,) + (3,) * ((depth - first) // 3)


def stages_of(count_y, count_z):
    if count_y * count_z <= 64:
        return (("py", "pz"),)
    return (("pz",), ("py",))


def radii_of(count_y, count_z):
    radii = [1]
    while 2 * radii[-1] < max(count_y, count_z) - 1:
        radii.append(2 * radii[-1])
    return tuple(radii)


def first_pair(column):
    return column * (column + 1) // 2


def kernel(
    groups,
    count_y,
    count_z,
    root_cells,
    start_hbm,
    x_hbm,
    y_hbm,
    z_hbm,
    shifts_hbm,
    field,
    triangle,
    splat,
    coef,
    coef_late,
    partial,
    row_source,
    known,
    shifts,
    *rest,
):
    stages = stages_of(count_y, count_z)
    row_buffers = rest[: len(stages)]
    load_sem, send_sem, recv_sem, coef_send, coef_recv, row_send, row_recv = rest[len(stages) :]
    depth = shifts.shape[0]
    count = depth + 1
    rows_y, rows_z, length = start_hbm.shape
    span_y, span_z = field.shape[1:3]
    half_y, half_z = (span_y - rows_y) // 2, (span_z - rows_z) // 2
    padded = triangle.shape[0]
    sizes = {"py": count_y, "pz": count_z}
    me = {"py": lax.axis_index("py"), "pz": lax.axis_index("pz")}
    me_y, me_z = me["py"], me["pz"]
    most = max(groups)

    has = []
    comes = []
    target = []
    for dy, dz in WAYS:
        ahead, behind = [], []
        for step, at, size in ((dy, me_y, count_y), (dz, me_z, count_z)):
            if step:
                up, down = at < size - 1, at > 0
                ahead.append(up if step > 0 else down)
                behind.append(down if step > 0 else up)
        has.append(functools.reduce(jnp.logical_and, ahead))
        comes.append(functools.reduce(jnp.logical_and, behind))
        target.append({"py": me_y + dy, "pz": me_z + dz})

    radii = radii_of(count_y, count_z) if len(stages) == 1 else ()

    def in_reach(radius):
        spans = [jnp.minimum(at + radius, size - 1) - jnp.maximum(at - radius, 0) + 1 for at, size in ((me_y, count_y), (me_z, count_z))]
        return spans[0] * spans[1] - 1

    def pass_on(step):
        radius = radii[step]

        def one(other, carry):
            other_y, other_z = lax.div(other, count_z), lax.rem(other, count_z)
            near = jnp.logical_and(jnp.abs(other_y - me_y) <= radius, jnp.abs(other_z - me_z) <= radius)
            near = jnp.logical_and(near, jnp.logical_or(other_y != me_y, other_z != me_z))
            pl.when(near)(
                lambda: pl.semaphore_signal(
                    known.at[step], inc=1, device_id={"py": other_y, "pz": other_z}, device_id_type=MESH
                )
            )
            return carry

        lax.fori_loop(0, count_y * count_z, one, 0)

    def heard(step):
        pl.semaphore_wait(known.at[step], in_reach(radii[step]))

    barrier = pltpu.get_barrier_semaphore()
    if radii:
        expected = in_reach(1)
        for way in range(8):
            pl.when(has[way])(
                lambda way=way: pl.semaphore_signal(
                    barrier, inc=1, device_id=target[way], device_id_type=MESH
                )
            )
    else:
        expected = count_y + count_z - 2
        for axis, size in sizes.items():
            def greet(away, carry):
                pl.semaphore_signal(
                    barrier, inc=1, device_id={axis: lax.rem(me[axis] + away, size)}, device_id_type=MESH
                )
                return carry

            lax.fori_loop(1, size, greet, 0)
        for way in range(4, 8):
            pl.when(has[way])(
                lambda way=way: pl.semaphore_signal(
                    barrier, inc=1, device_id=target[way], device_id_type=MESH
                )
            )
            expected = expected + jnp.where(comes[way], 1, 0)

    own = (pl.ds(half_y, rows_y), pl.ds(0, rows_z))
    loads = [
        pltpu.make_async_copy(source, place.at[own], load_sem.at[i])
        for i, (source, place) in enumerate(
            (
                (start_hbm, field.at[0]),
                (z_hbm, coef.at[AT_Z]),
                (y_hbm, coef.at[AT_Y]),
                (x_hbm, coef.at[AT_X]),
            )
        )
    ]
    loads.append(pltpu.make_async_copy(shifts_hbm, shifts, load_sem.at[4]))
    for load in loads:
        load.start()

    def ends_y(step, first, last):
        if step > 0:
            return pl.ds(half_y + rows_y - last, last - first), pl.ds(half_y - last, last - first)
        if step < 0:
            return pl.ds(half_y + first, last - first), pl.ds(half_y + rows_y + first, last - first)
        return pl.ds(half_y, rows_y), pl.ds(half_y, rows_y)

    def ends_z(step, first, last):
        if step > 0:
            return pl.ds(rows_z - last, last - first), pl.ds(span_z - last, last - first)
        if step < 0:
            return pl.ds(first, last - first), pl.ds(rows_z + first, last - first)
        return pl.ds(0, rows_z), pl.ds(0, rows_z)

    def copy(array, which, way, y_band, z_band, sends, recvs, index, place=None):
        dy, dz = WAYS[way]
        from_y, to_y = ends_y(dy, *y_band)
        from_z, to_z = ends_z(dz, *z_band)
        return way, pltpu.make_async_remote_copy(
            src_ref=array.at[which, from_y, from_z],
            dst_ref=(array if place is None else place).at[which, to_y, to_z],
            send_sem=sends.at[index],
            recv_sem=recvs.at[index],
            device_id=target[way],
            device_id_type=MESH,
        )

    def start_all(copies):
        for way, each in copies:
            pl.when(has[way])(lambda each=each: each.start())

    def arrive_all(copies):
        for way, each in copies:
            pl.when(comes[way])(lambda each=each: each.wait_recv())

    def leave_all(copies):
        for way, each in copies:
            pl.when(has[way])(lambda each=each: each.wait_send())

    def field_copies(group):
        slot, reach = sum(groups[:group]), groups[group]
        bands = [(0, reach if way < 4 else reach - 1) for way in range(8 if reach > 1 else 4)]
        return [
            copy(field, slot, way, band, band, send_sem, recv_sem, group * 8 + way)
            for way, band in enumerate(bands)
        ]

    coef_parts = []

    def coef_band(before, after):
        copies = []

        def add(which, way, y_band, z_band, place=None):
            if y_band[1] > y_band[0] and z_band[1] > z_band[0]:
                index = len(coef_parts)
                coef_parts.append(index)
                copies.append(copy(coef, which, way, y_band, z_band, coef_send, coef_recv, index, place))

        for way, (dy, dz) in enumerate(WAYS):
            if way < 2:
                low = (max(before - 1, 0), after - 1)
                if dy < 0:
                    add(pl.ds(0, 3), way, low, low)
                else:
                    add(AT_Y, way, (before, after), (0, 1))
                    add(pl.ds(AT_Z, 2), way, low, (0, 1))
                continue
            place = coef_late if before else coef
            if way < 4:
                low = (0, after - 1)
                if dz < 0:
                    add(pl.ds(0, 3), way, low, low, place)
                else:
                    add(AT_Z, way, (0, 1), (0, after), place)
                    add(pl.ds(AT_X, 2), way, (0, 1), low, place)
            else:
                wide, narrow = (0, max(after - 1, 0)), (0, max(after - 2, 0))
                if dy == dz:
                    band = wide if dy > 0 else narrow
                    add(pl.ds(0, 3), way, band, band, place)
                else:
                    add(AT_Y if dy > 0 else AT_Z, way, wide, wide, place)
                    add(pl.ds(AT_Z if dy > 0 else AT_X, 2), way, narrow, narrow, place)
        return copies

    fields = [field_copies(group) for group in range(len(groups))]
    early, late = coef_band(0, groups[0]), coef_band(groups[0], most) if most > groups[0] else []

    for load in loads:
        load.wait()
    pl.semaphore_wait(barrier, expected)
    start_all(fields[0])
    start_all(early)
    start_all(late)
    if radii:
        pass_on(0)

    def clear(block_y, block_z):
        shape = (block_y[1], block_z[1], length)
        where = (pl.ds(*block_y), pl.ds(*block_z))

        def one(piece, carry):
            coef[(piece, *where)] = jnp.zeros(shape, jnp.float32)
            coef_late[(piece, *where)] = jnp.zeros(shape, jnp.float32)
            return carry

        lax.fori_loop(0, 3, one, 0)
        for group in range(len(groups)):
            field[(sum(groups[:group]), *where)] = jnp.zeros(shape, jnp.float32)

    pl.when(me_y == 0)(lambda: clear((0, half_y), (0, span_z)))
    pl.when(me_y == count_y - 1)(lambda: clear((half_y + rows_y, half_y), (0, span_z)))
    pl.when(me_z == 0)(lambda: clear((0, span_y), (rows_z + half_z, half_z)))
    pl.when(me_z == count_z - 1)(lambda: clear((0, span_y), (rows_z, half_z)))

    pieces = range(length // LANES)
    last_piece = length // LANES - 1
    lane = lax.broadcasted_iota(jnp.int32, (rows_z, LANES), 1)
    sub = lax.broadcasted_iota(jnp.int32, (rows_z, LANES), 0)
    right_edge, left_edge = lane == LANES - 1, lane == 0
    top_row, bottom_row = sub == rows_z - 1, sub == 0
    inside_z = jnp.where(
        sub < half_z,
        jnp.where(me_z < count_z - 1, 1.0, 0.0),
        jnp.where(me_z > 0, 1.0, 0.0),
    )
    scale_below = jnp.where(me_y > 0, step_scale, 0.0)
    scale_above = jnp.where(me_y < count_y - 1, step_scale, 0.0)

    def shifted(rows):
        ahead = [pltpu.roll(row, LANES - 1, 1) for row in rows]
        behind = [pltpu.roll(row, 1, 1) for row in rows]
        return (
            [jnp.where(right_edge, ahead[x + 1] if x < last_piece else 0.0, ahead[x]) for x in pieces],
            [jnp.where(left_edge, behind[x - 1] if x else 0.0, behind[x]) for x in pieces],
        )

    def turn_x(array, first, last, tile):
        for y in range(first, last):
            where = [(y, pl.ds(tile * rows_z, rows_z), pl.ds(x * LANES, LANES)) for x in pieces]
            for at, behind in zip(where, shifted([array[(AT_X, *at)] for at in where])[1]):
                array[(AT_BEHIND, *at)] = behind

    def level(group, step):
        slot = sum(groups[:group]) + step
        left = groups[group] - step - 1
        shift = shifts[slot]
        tiles = (0, 1) if left else (0,)

        def at(tile, x):
            return pl.ds(tile * rows_z, rows_z), pl.ds(x * LANES, LANES)

        def value(y, tile, x):
            return field[(slot, y, *at(tile, x))]

        beyond = coef_late if group else coef

        def factor(which, y, tile, x):
            return (beyond if tile else coef)[(which, y, *at(tile, x))]

        def edge(array, which, y, z, x):
            return array[which, y, pl.ds(z, 1), pl.ds(x * LANES, LANES)]

        def part_z(y, x, outer):
            if outer:
                rows = [value(y, tile, x) for tile in tiles]
                turned = [pltpu.roll(row, rows_z - 1, 0) for row in rows]
                flux = [
                    factor(AT_Z, y, tile, x)
                    * (rows[tile] - jnp.where(top_row, turned[1 - tile], turned[tile]))
                    for tile in tiles
                ]
                turned = [pltpu.roll(each, 1, 0) for each in flux]
                return [
                    flux[tile] - jnp.where(bottom_row, turned[1 - tile], turned[tile]) for tile in tiles
                ]
            row = value(y, 0, x)
            up = jnp.where(top_row, edge(field, slot, y, rows_z, x), pltpu.roll(row, rows_z - 1, 0))
            flux = factor(AT_Z, y, 0, x) * (row - up)
            below = edge(beyond, AT_Z, y, span_z - 1, x) * (edge(field, slot, y, span_z - 1, x) - row[0:1, :])
            return [flux - jnp.where(bottom_row, below, pltpu.roll(flux, 1, 0))]

        def part_x(y, tile):
            rows = [value(y, tile, x) for x in pieces]
            ahead, behind = shifted(rows)
            return [
                factor(AT_X, y, tile, x) * (rows[x] - ahead[x])
                + factor(AT_BEHIND, y, tile, x) * (rows[x] - behind[x])
                for x in pieces
            ]

        def flux_y(y, tile, x):
            return factor(AT_Y, y, tile, x) * (value(y, tile, x) - value(y + 1, tile, x))

        first, last = half_y - left, half_y + rows_y + left

        carried = {}
        for y in range(first, last):
            scale = step_scale if half_y <= y < half_y + rows_y else scale_below if y < half_y else scale_above
            here = tiles[:1] if left and y in (first, last - 1) else tiles
            along_x = [part_x(y, tile) for tile in here]
            along_z = [part_z(y, x, len(here) > 1) for x in pieces]
            for tile in here:
                scale_tile = scale * inside_z if tile else scale
                for x in pieces:
                    flux = flux_y(y, tile, x)
                    below = carried[tile, x] if (tile, x) in carried else flux_y(y - 1, tile, x)
                    change = (flux - below) - shift * value(y, tile, x)
                    fresh = (along_x[tile][x] + along_z[x][tile]) + change
                    field[(slot + 1, y, *at(tile, x))] = fresh * scale_tile
                    carried[tile, x] = flux

    def gram(columns):
        pairs = [(i, j) for j in columns for i in range(j + 1)]

        def plane(y, totals):
            totals = list(totals)
            for x in range(0, length, LANES):
                pieces = [field[i, half_y + y, pl.ds(0, rows_z), pl.ds(x, LANES)] for i in range(max(columns) + 1)]
                for p, (i, j) in enumerate(pairs):
                    totals[p] = totals[p] + pieces[i] * pieces[j]
            return tuple(totals)

        zero = jnp.zeros((SUBLANES, LANES), jnp.float32)
        totals = lax.fori_loop(0, rows_y, plane, (zero,) * len(pairs))
        for (i, j), total in zip(pairs, totals):
            partial[pl.ds((first_pair(j) + i) * SUBLANES, SUBLANES), :] = total

    pairs = first_pair(count)
    many = partial.shape[0] // SUBLANES
    for at in range(pairs, many):
        partial[pl.ds(at * SUBLANES, SUBLANES), :] = jnp.zeros((SUBLANES, LANES), jnp.float32)

    turn_x(coef, half_y, half_y + rows_y, 0)
    for group, applications in enumerate(groups):
        if group:
            start_all(fields[group])
        if group == 1:
            arrive_all(late)
            turn_x(coef, half_y - most + 1, half_y - groups[0] + 1, 0)
            turn_x(coef, half_y + rows_y + groups[0] - 1, half_y + rows_y + most - 1, 0)
            turn_x(coef_late, half_y - most + 2, half_y + rows_y + most - 2, 1)
        if 0 < group < len(radii):
            heard(group - 1)
            pass_on(group)
        if group:
            gram(range(0 if group == 1 else sum(groups[: group - 1]) + 1, sum(groups[:group]) + 1))
        arrive_all(fields[group])
        if group == 0:
            arrive_all(early)
        if group == 0:
            reach = applications - 1
            turn_x(coef, half_y - reach, half_y, 0)
            turn_x(coef, half_y + rows_y, half_y + rows_y + reach, 0)
            turn_x(coef, half_y - reach + 1, half_y + rows_y + reach - 1, 1)
        for step in range(applications):
            level(group, step)
    gram(range(sum(groups[:-1]) + 1, count))

    high, low = sum_pairs(
        [
            (partial[pl.ds(s, many, stride=SUBLANES), :], jnp.zeros((many, LANES), jnp.float32))
            for s in range(SUBLANES)
        ]
    )
    fill = jnp.zeros((LANES // 2 - many, LANES), jnp.float32)
    turned = jnp.concatenate([high, fill, low, fill], axis=0).T
    total = sum_rows([turned[y : y + SUBLANES] for y in range(0, LANES, SUBLANES)])
    if radii:
        heard(len(radii) - 1)
    sent = []
    for stage, axes in enumerate(stages):
        buffer = row_buffers[stage]
        size = math.prod(sizes[axis] for axis in axes)
        index = functools.reduce(lambda at, axis: at * sizes[axis] + me[axis], axes, 0)
        row_source[stage] = packed(*total)
        if buffer.shape[0] > size:
            buffer[pl.ds(size, buffer.shape[0] - size), :] = jnp.zeros(
                (buffer.shape[0] - size, LANES), jnp.float32
            )

        def send(away, carry):
            other = lax.rem(index + away, size)
            device = {}
            for axis in reversed(axes):
                device[axis] = lax.rem(other, sizes[axis])
                other = lax.div(other, sizes[axis])
            pltpu.make_async_remote_copy(
                src_ref=row_source.at[stage, pl.ds(0, 1)],
                dst_ref=buffer.at[pl.ds(index, 1)],
                send_sem=row_send.at[stage],
                recv_sem=row_recv.at[stage],
                device_id=device,
                device_id_type=MESH,
            ).start()
            return carry

        lax.fori_loop(1, size, send, 0)
        buffer[pl.ds(index, 1), :] = row_source[stage, pl.ds(0, 1), :]
        if stage == 0:
            for copies in (*fields, early, late):
                leave_all(copies)
        others = buffer.at[pl.ds(0, size - 1)]
        pltpu.make_async_copy(others, others, row_recv.at[stage]).wait()
        sent.append(pltpu.make_async_copy(others, others, row_send.at[stage]))
        rows = [buffer[pl.ds(y, SUBLANES), :] for y in range(0, buffer.shape[0], SUBLANES)]
        total = sum_rows(rows)

    total = fold(total)
    high, low = {}, {}
    for j in range(count):
        for i in range(j + 1):
            p = first_pair(j) + i
            high[i, j], low[i, j] = (
                jnp.broadcast_to(piece[:, p : p + 1], (SUBLANES, LANES)) for piece in total
            )
    square_sub = lax.broadcasted_iota(jnp.int32, (padded, LANES), 0)
    square_lane = lax.broadcasted_iota(jnp.int32, (padded, LANES), 1)
    tri = jnp.zeros((padded, LANES), jnp.float32)
    for k in range(count):
        for j in range(k, count):
            high[k, j], low[k, j] = renormal((high[k, j], low[k, j]))
        d_high, d_low = high[k, k], low[k, k]
        inverse = 1.0 / d_high
        root = jnp.sqrt(d_high) * root_cells
        scale = 1.0 / root
        for j in range(k, count):
            value = high[k, j] * scale
            splat[k * count + j] = root * inverse if j == k else value
            here = jnp.logical_and(square_sub == k, square_lane == j)
            tri = jnp.where(here, jnp.concatenate([value] * (padded // SUBLANES), axis=0), tri)
        halves = {j: split(high[k, j]) for j in range(k, count)}
        for i in range(k + 1, count):
            lead = high[k, i] * inverse
            lead_high, lead_low = split(lead)

            def times(j):
                product = lead * high[k, j]
                big, small = halves[j]
                error = ((lead_high * big - product) + lead_high * small + lead_low * big) + lead_low * small
                return product, error

            product, error = times(k)
            minor = (((high[k, i] - product) - error) + (low[k, i] - lead * d_low)) * inverse
            for j in range(i, count):
                product, error = times(j)
                error = error + (high[k, j] * minor + low[k, j] * lead)
                rest_high, rest_low = two_sum(high[i, j], -product)
                high[i, j], low[i, j] = rest_high, rest_low + (low[i, j] - error)
    triangle[...] = tri
    for each in sent:
        each.wait()


def substitute(basis, factor, splat, out, triangle, solved_rows, small, sems, small_sem):
    count, rows_y, rows_z, length = solved_rows.shape
    first = (basis.shape[1] - rows_y) // 2
    small[...] = factor[:count, :count]
    copies = [pltpu.make_async_copy(small, triangle, small_sem)]
    copies[0].start()

    def plane(y, carry):
        for x in range(0, length, LANES):
            solved = []
            for i in range(count):
                value = basis[i, first + y, pl.ds(0, rows_z), x : x + LANES]
                for k in range(i):
                    value = value - splat[k * count + i] * solved[k]
                value = value * splat[i * count + i]
                solved_rows[i, y, :, x : x + LANES] = value
                solved.append(value)
        return carry

    part = rows_y // 4
    for p in range(4):
        lax.fori_loop(p * part, (p + 1) * part, plane, 0, unroll=2)
        rows = pl.ds(p * part, part)
        copies.append(pltpu.make_async_copy(solved_rows.at[:, rows], out.at[:, rows], sems.at[p]))
        copies[-1].start()
    for each in copies:
        each.wait()


def on_device(start, coef_x, coef_y, coef_z, shifts):
    rows_y, rows_z, length = start.shape
    depth = shifts.shape[0]
    count = depth + 1
    padded = (count + SUBLANES - 1) // SUBLANES * SUBLANES
    count_y, count_z = lax.axis_size("py"), lax.axis_size("pz")
    cells = length * rows_y * rows_z * count_y * count_z
    groups = plan(depth)
    span_y, span_z = rows_y + 8, rows_z + 8
    stages = stages_of(count_y, count_z)
    sizes = {"py": count_y, "pz": count_z}
    members = [math.prod(sizes[axis] for axis in axes) for axes in stages]
    whole = pl.BlockSpec(memory_space=pltpu.VMEM)
    many = (first_pair(count) + SUBLANES - 1) // SUBLANES * SUBLANES
    pltpu_f32 = lambda *shape: pltpu.VMEM(shape, jnp.float32)
    dma = pltpu.SemaphoreType.DMA
    vmem_limit = 2**26 - 4 * (count * span_y * span_z * length) - 2**19
    anywhere = pl.BlockSpec(memory_space=pl.ANY)
    basis, factor, splat = pl.pallas_call(
        functools.partial(kernel, groups, count_y, count_z, math.sqrt(cells)),
        out_shape=(
            pltpu_f32(count, span_y, span_z, length),
            pltpu_f32(padded, LANES),
            pltpu_f32(count * count, SUBLANES, LANES),
        ),
        in_specs=[anywhere] * 5,
        out_specs=(whole, whole, whole),
        scratch_shapes=[
            pltpu_f32(4, span_y, span_z, length),
            pltpu_f32(4, span_y, span_z, length),
            pltpu_f32(many * SUBLANES, LANES),
            pltpu_f32(len(stages), SUBLANES, LANES),
            pltpu.SemaphoreType.REGULAR((8,)),
            pltpu.SMEM((depth,), jnp.float32),
            *[pltpu_f32((n + SUBLANES - 1) // SUBLANES * SUBLANES, LANES) for n in members],
            dma((5,)),
            dma((len(groups) * 8,)),
            dma((len(groups) * 8,)),
            dma((32,)),
            dma((32,)),
            dma((len(stages),)),
            dma((len(stages),)),
        ],
        compiler_params=pltpu.CompilerParams(
            collective_id=0, has_side_effects=True, vmem_limit_bytes=vmem_limit
        ),
    )(start, coef_x, coef_y, coef_z, shifts)
    basis = pltpu.with_memory_space_constraint(basis, pltpu.VMEM)
    factor = pltpu.with_memory_space_constraint(factor, pltpu.VMEM)
    splat = pltpu.with_memory_space_constraint(splat, pltpu.VMEM)
    return pl.pallas_call(
        substitute,
        out_shape=(
            jax.ShapeDtypeStruct((count, rows_y, rows_z, length), jnp.float32),
            jax.ShapeDtypeStruct((count, count), jnp.float32),
        ),
        in_specs=[whole, whole, whole],
        out_specs=(anywhere, anywhere),
        scratch_shapes=[pltpu_f32(count, rows_y, rows_z, length), pltpu_f32(count, count), dma((4,)), dma],
        compiler_params=pltpu.CompilerParams(vmem_limit_bytes=vmem_limit),
    )(basis, factor, splat)


def solution(mesh):
    placed = (
        P("py", "pz", None),
        P("py", "pz", None),
        P("py", "pz", None),
        P("py", "pz", None),
        P(),
    )
    return jax.shard_map(
        on_device,
        mesh=mesh,
        in_specs=placed,
        out_specs=(P(None, "py", "pz", None), P()),
        check_vma=False,
    )
```

```python
import functools
import math

import jax
import jax.numpy as jnp
from jax import lax
from jax.experimental import pallas as pl
from jax.experimental.pallas import tpu as pltpu
from jax.sharding import PartitionSpec as P

step_scale = 0.125
MESH = pl.DeviceIdType.MESH
LANES = 128
SUBLANES = 8
WAYS = ((1, 0), (-1, 0), (0, 1), (0, -1), (1, 1), (1, -1), (-1, 1), (-1, -1))


def two_sum(a, b):
    total = a + b
    virtual = total - a
    return total, (a - (total - virtual)) + (b - virtual)


def split(a):
    scaled = a * 4097.0
    high = scaled - (scaled - a)
    return high, a - high


def two_product(a, b):
    product = a * b
    a_high, a_low = split(a)
    b_high, b_low = split(b)
    error = ((a_high * b_high - product) + a_high * b_low + a_low * b_high) + a_low * b_low
    return product, error


def pair_add(a, b):
    total, error = two_sum(a[0], b[0])
    return total, error + (a[1] + b[1])


def renormal(a):
    total = a[0] + a[1]
    return total, a[1] - (total - a[0])


def tree(parts):
    while len(parts) > 1:
        rest = parts[len(parts) // 2 * 2 :]
        parts = [pair_add(parts[i], parts[i + 1]) for i in range(0, len(parts) - 1, 2)] + rest
    return parts[0]


AT_Z, AT_X, AT_Y, AT_BEHIND = range(4)


def sum_pairs(parts):
    while len(parts) > 1:
        rest = parts[len(parts) // 2 * 2 :]
        added = []
        for i in range(0, len(parts) - 1, 2):
            total, error = two_sum(parts[i][0], parts[i + 1][0])
            added.append((total, error + (parts[i][1] + parts[i + 1][1])))
        parts = added + rest
    return parts[0]


def sum_rows(tiles):
    zero = jnp.zeros_like(tiles[0])
    total = sum_pairs([(tile, zero) for tile in tiles])
    shift = SUBLANES // 2
    while shift:
        total = pair_add(total, tuple(pltpu.roll(piece, shift, 0) for piece in total))
        shift //= 2
    return total


def fold(total):
    lead, minor = total
    return renormal((lead, minor + pltpu.roll(lead + minor, LANES // 2, 1)))


def packed(lead, minor):
    lane = lax.broadcasted_iota(jnp.int32, lead.shape, 1)
    return jnp.where(lane < LANES // 2, lead, (lead + minor) + pltpu.roll(minor, LANES // 2, 1))


def plan(depth):
    first = depth % 3 or 3
    return (first,) + (3,) * ((depth - first) // 3)


def stages_of(count_y, count_z):
    if count_y * count_z <= 64:
        return (("py", "pz"),)
    return (("pz",), ("py",))


def radii_of(count_y, count_z):
    radii = [1]
    while 2 * radii[-1] < max(count_y, count_z) - 1:
        radii.append(2 * radii[-1])
    return tuple(radii)


def first_pair(column):
    return column * (column + 1) // 2


def kernel(
    groups,
    count_y,
    count_z,
    root_cells,
    start_hbm,
    x_hbm,
    y_hbm,
    z_hbm,
    shifts_hbm,
    field,
    triangle,
    splat,
    coef,
    coef_late,
    partial,
    row_source,
    known,
    shifts,
    *rest,
):
    stages = stages_of(count_y, count_z)
    row_buffers = rest[: len(stages)]
    load_sem, send_sem, recv_sem, coef_send, coef_recv, row_send, row_recv = rest[len(stages) :]
    depth = shifts.shape[0]
    count = depth + 1
    rows_y, rows_z, length = start_hbm.shape
    span_y, span_z = field.shape[1:3]
    half_y, half_z = (span_y - rows_y) // 2, (span_z - rows_z) // 2
    padded = triangle.shape[0]
    sizes = {"py": count_y, "pz": count_z}
    me = {"py": lax.axis_index("py"), "pz": lax.axis_index("pz")}
    me_y, me_z = me["py"], me["pz"]
    most = max(groups)

    has = []
    comes = []
    target = []
    for dy, dz in WAYS:
        ahead, behind = [], []
        for step, at, size in ((dy, me_y, count_y), (dz, me_z, count_z)):
            if step:
                up, down = at < size - 1, at > 0
                ahead.append(up if step > 0 else down)
                behind.append(down if step > 0 else up)
        has.append(functools.reduce(jnp.logical_and, ahead))
        comes.append(functools.reduce(jnp.logical_and, behind))
        target.append({"py": me_y + dy, "pz": me_z + dz})

    radii = radii_of(count_y, count_z) if len(stages) == 1 else ()

    def in_reach(radius):
        spans = [jnp.minimum(at + radius, size - 1) - jnp.maximum(at - radius, 0) + 1 for at, size in ((me_y, count_y), (me_z, count_z))]
        return spans[0] * spans[1] - 1

    def pass_on(step):
        radius = radii[step]
        if radius == 1:
            for way in range(8):
                pl.when(has[way])(
                    lambda way=way: pl.semaphore_signal(
                        known.at[step], inc=1, device_id=target[way], device_id_type=MESH
                    )
                )
            return

        def one(other, carry):
            other_y, other_z = lax.div(other, count_z), lax.rem(other, count_z)
            near = jnp.logical_and(jnp.abs(other_y - me_y) <= radius, jnp.abs(other_z - me_z) <= radius)
            near = jnp.logical_and(near, jnp.logical_or(other_y != me_y, other_z != me_z))
            pl.when(near)(
                lambda: pl.semaphore_signal(
                    known.at[step], inc=1, device_id={"py": other_y, "pz": other_z}, device_id_type=MESH
                )
            )
            return carry

        lax.fori_loop(0, count_y * count_z, one, 0)

    def heard(step):
        pl.semaphore_wait(known.at[step], in_reach(radii[step]))

    barrier = pltpu.get_barrier_semaphore()
    if radii:
        expected = in_reach(1)
        for way in range(8):
            pl.when(has[way])(
                lambda way=way: pl.semaphore_signal(
                    barrier, inc=1, device_id=target[way], device_id_type=MESH
                )
            )
    else:
        expected = count_y + count_z - 2
        for axis, size in sizes.items():
            def greet(away, carry):
                pl.semaphore_signal(
                    barrier, inc=1, device_id={axis: lax.rem(me[axis] + away, size)}, device_id_type=MESH
                )
                return carry

            lax.fori_loop(1, size, greet, 0)
        for way in range(4, 8):
            pl.when(has[way])(
                lambda way=way: pl.semaphore_signal(
                    barrier, inc=1, device_id=target[way], device_id_type=MESH
                )
            )
            expected = expected + jnp.where(comes[way], 1, 0)

    own = (pl.ds(half_y, rows_y), pl.ds(0, rows_z))
    loads = [
        pltpu.make_async_copy(source, place.at[own], load_sem.at[i])
        for i, (source, place) in enumerate(
            (
                (start_hbm, field.at[0]),
                (z_hbm, coef.at[AT_Z]),
                (y_hbm, coef.at[AT_Y]),
                (x_hbm, coef.at[AT_X]),
            )
        )
    ]
    loads.append(pltpu.make_async_copy(shifts_hbm, shifts, load_sem.at[4]))
    for load in loads:
        load.start()

    def ends_y(step, first, last):
        if step > 0:
            return pl.ds(half_y + rows_y - last, last - first), pl.ds(half_y - last, last - first)
        if step < 0:
            return pl.ds(half_y + first, last - first), pl.ds(half_y + rows_y + first, last - first)
        return pl.ds(half_y, rows_y), pl.ds(half_y, rows_y)

    def ends_z(step, first, last):
        if step > 0:
            return pl.ds(rows_z - last, last - first), pl.ds(span_z - last, last - first)
        if step < 0:
            return pl.ds(first, last - first), pl.ds(rows_z + first, last - first)
        return pl.ds(0, rows_z), pl.ds(0, rows_z)

    def copy(array, which, way, y_band, z_band, sends, recvs, index, place=None):
        dy, dz = WAYS[way]
        from_y, to_y = ends_y(dy, *y_band)
        from_z, to_z = ends_z(dz, *z_band)
        return way, pltpu.make_async_remote_copy(
            src_ref=array.at[which, from_y, from_z],
            dst_ref=(array if place is None else place).at[which, to_y, to_z],
            send_sem=sends.at[index],
            recv_sem=recvs.at[index],
            device_id=target[way],
            device_id_type=MESH,
        )

    def start_all(copies):
        for way, each in copies:
            pl.when(has[way])(lambda each=each: each.start())

    def arrive_all(copies):
        for way, each in copies:
            pl.when(comes[way])(lambda each=each: each.wait_recv())

    def leave_all(copies):
        for way, each in copies:
            pl.when(has[way])(lambda each=each: each.wait_send())

    def field_copies(group):
        slot, reach = sum(groups[:group]), groups[group]
        bands = [(0, reach if way < 4 else reach - 1) for way in range(8 if reach > 1 else 4)]
        return [
            copy(field, slot, way, band, band, send_sem, recv_sem, group * 8 + way)
            for way, band in enumerate(bands)
        ]

    coef_parts = []

    def coef_band(before, after):
        copies = []

        def add(which, way, y_band, z_band, place=None):
            if y_band[1] > y_band[0] and z_band[1] > z_band[0]:
                index = len(coef_parts)
                coef_parts.append(index)
                copies.append(copy(coef, which, way, y_band, z_band, coef_send, coef_recv, index, place))

        for way, (dy, dz) in enumerate(WAYS):
            if way < 2:
                low = (max(before - 1, 0), after - 1)
                if dy < 0:
                    add(pl.ds(0, 3), way, low, low)
                else:
                    add(AT_Y, way, (before, after), (0, 1))
                    add(pl.ds(AT_Z, 2), way, low, (0, 1))
                continue
            place = coef_late if before else coef
            if way < 4:
                low = (0, after - 1)
                if dz < 0:
                    add(pl.ds(0, 3), way, low, low, place)
                else:
                    add(AT_Z, way, (0, 1), (0, after), place)
                    add(pl.ds(AT_X, 2), way, (0, 1), low, place)
            else:
                wide, narrow = (0, max(after - 1, 0)), (0, max(after - 2, 0))
                if dy == dz:
                    band = wide if dy > 0 else narrow
                    add(pl.ds(0, 3), way, band, band, place)
                else:
                    add(AT_Y if dy > 0 else AT_Z, way, wide, wide, place)
                    add(pl.ds(AT_Z if dy > 0 else AT_X, 2), way, narrow, narrow, place)
        return copies

    fields = [field_copies(group) for group in range(len(groups))]
    early, late = coef_band(0, groups[0]), coef_band(groups[0], most) if most > groups[0] else []

    for load in loads:
        load.wait()
    pl.semaphore_wait(barrier, expected)
    start_all(fields[0][:2])
    start_all([each for each in early if each[0] < 2])
    start_all(fields[0][2:])
    start_all([each for each in early if each[0] >= 2])
    start_all(late)
    if radii:
        pass_on(0)

    def clear(block_y, block_z):
        shape = (block_y[1], block_z[1], length)
        where = (pl.ds(*block_y), pl.ds(*block_z))

        def one(piece, carry):
            coef[(piece, *where)] = jnp.zeros(shape, jnp.float32)
            coef_late[(piece, *where)] = jnp.zeros(shape, jnp.float32)
            return carry

        lax.fori_loop(0, 3, one, 0)
        for group in range(len(groups)):
            field[(sum(groups[:group]), *where)] = jnp.zeros(shape, jnp.float32)

    pl.when(me_y == 0)(lambda: clear((0, half_y), (0, span_z)))
    pl.when(me_y == count_y - 1)(lambda: clear((half_y + rows_y, half_y), (0, span_z)))
    pl.when(me_z == 0)(lambda: clear((0, span_y), (rows_z + half_z, half_z)))
    pl.when(me_z == count_z - 1)(lambda: clear((0, span_y), (rows_z, half_z)))

    pieces = range(length // LANES)
    last_piece = length // LANES - 1
    lane = lax.broadcasted_iota(jnp.int32, (rows_z, LANES), 1)
    sub = lax.broadcasted_iota(jnp.int32, (rows_z, LANES), 0)
    right_edge, left_edge = lane == LANES - 1, lane == 0
    top_row, bottom_row = sub == rows_z - 1, sub == 0
    inside_z = jnp.where(
        sub < half_z,
        jnp.where(me_z < count_z - 1, 1.0, 0.0),
        jnp.where(me_z > 0, 1.0, 0.0),
    )
    scale_below = jnp.where(me_y > 0, step_scale, 0.0)
    scale_above = jnp.where(me_y < count_y - 1, step_scale, 0.0)

    def shifted(rows):
        ahead = [pltpu.roll(row, LANES - 1, 1) for row in rows]
        behind = [pltpu.roll(row, 1, 1) for row in rows]
        return (
            [jnp.where(right_edge, ahead[x + 1] if x < last_piece else 0.0, ahead[x]) for x in pieces],
            [jnp.where(left_edge, behind[x - 1] if x else 0.0, behind[x]) for x in pieces],
        )

    def turn_x(array, first, last, tile):
        for y in range(first, last):
            where = [(y, pl.ds(tile * rows_z, rows_z), pl.ds(x * LANES, LANES)) for x in pieces]
            for at, behind in zip(where, shifted([array[(AT_X, *at)] for at in where])[1]):
                array[(AT_BEHIND, *at)] = behind

    def level(group, step):
        slot = sum(groups[:group]) + step
        left = groups[group] - step - 1
        shift = shifts[slot]
        tiles = (0, 1) if left else (0,)

        def at(tile, x):
            return pl.ds(tile * rows_z, rows_z), pl.ds(x * LANES, LANES)

        def value(y, tile, x):
            return field[(slot, y, *at(tile, x))]

        beyond = coef_late if group else coef

        def factor(which, y, tile, x):
            return (beyond if tile else coef)[(which, y, *at(tile, x))]

        def edge(array, which, y, z, x):
            return array[which, y, pl.ds(z, 1), pl.ds(x * LANES, LANES)]

        def part_z(y, x, outer):
            if outer:
                rows = [value(y, tile, x) for tile in tiles]
                turned = [pltpu.roll(row, rows_z - 1, 0) for row in rows]
                flux = [
                    factor(AT_Z, y, tile, x)
                    * (rows[tile] - jnp.where(top_row, turned[1 - tile], turned[tile]))
                    for tile in tiles
                ]
                turned = [pltpu.roll(each, 1, 0) for each in flux]
                return [
                    flux[tile] - jnp.where(bottom_row, turned[1 - tile], turned[tile]) for tile in tiles
                ]
            row = value(y, 0, x)
            up = jnp.where(top_row, edge(field, slot, y, rows_z, x), pltpu.roll(row, rows_z - 1, 0))
            flux = factor(AT_Z, y, 0, x) * (row - up)
            below = edge(beyond, AT_Z, y, span_z - 1, x) * (edge(field, slot, y, span_z - 1, x) - row[0:1, :])
            return [flux - jnp.where(bottom_row, below, pltpu.roll(flux, 1, 0))]

        def part_x(y, tile):
            rows = [value(y, tile, x) for x in pieces]
            ahead, behind = shifted(rows)
            return [
                factor(AT_X, y, tile, x) * (rows[x] - ahead[x])
                + factor(AT_BEHIND, y, tile, x) * (rows[x] - behind[x])
                for x in pieces
            ]

        def flux_y(y, tile, x):
            return factor(AT_Y, y, tile, x) * (value(y, tile, x) - value(y + 1, tile, x))

        first, last = half_y - left, half_y + rows_y + left

        carried = {}
        for y in range(first, last):
            scale = step_scale if half_y <= y < half_y + rows_y else scale_below if y < half_y else scale_above
            here = tiles[:1] if left and y in (first, last - 1) else tiles
            along_x = [part_x(y, tile) for tile in here]
            along_z = [part_z(y, x, len(here) > 1) for x in pieces]
            for tile in here:
                scale_tile = scale * inside_z if tile else scale
                for x in pieces:
                    flux = flux_y(y, tile, x)
                    below = carried[tile, x] if (tile, x) in carried else flux_y(y - 1, tile, x)
                    change = (flux - below) - shift * value(y, tile, x)
                    fresh = (along_x[tile][x] + along_z[x][tile]) + change
                    field[(slot + 1, y, *at(tile, x))] = fresh * scale_tile
                    carried[tile, x] = flux

    def gram(columns):
        pairs = [(i, j) for j in columns for i in range(j + 1)]

        def plane(y, totals):
            totals = list(totals)
            for x in range(0, length, LANES):
                pieces = [field[i, half_y + y, pl.ds(0, rows_z), pl.ds(x, LANES)] for i in range(max(columns) + 1)]
                for p, (i, j) in enumerate(pairs):
                    totals[p] = totals[p] + pieces[i] * pieces[j]
            return tuple(totals)

        zero = jnp.zeros((SUBLANES, LANES), jnp.float32)
        totals = lax.fori_loop(0, rows_y, plane, (zero,) * len(pairs))
        for (i, j), total in zip(pairs, totals):
            partial[pl.ds((first_pair(j) + i) * SUBLANES, SUBLANES), :] = total

    pairs = first_pair(count)
    many = partial.shape[0] // SUBLANES
    for at in range(pairs, many):
        partial[pl.ds(at * SUBLANES, SUBLANES), :] = jnp.zeros((SUBLANES, LANES), jnp.float32)

    turn_x(coef, half_y, half_y + rows_y, 0)
    for group, applications in enumerate(groups):
        if group:
            start_all(fields[group])
        if group == 1:
            arrive_all(late)
            turn_x(coef, half_y - most + 1, half_y - groups[0] + 1, 0)
            turn_x(coef, half_y + rows_y + groups[0] - 1, half_y + rows_y + most - 1, 0)
            turn_x(coef_late, half_y - most + 2, half_y + rows_y + most - 2, 1)
        if 0 < group < len(radii):
            heard(group - 1)
            pass_on(group)
        if group:
            gram(range(0 if group == 1 else sum(groups[: group - 1]) + 1, sum(groups[:group]) + 1))
        arrive_all(fields[group])
        if group == 0:
            arrive_all(early)
        if group == 0:
            reach = applications - 1
            turn_x(coef, half_y - reach, half_y, 0)
            turn_x(coef, half_y + rows_y, half_y + rows_y + reach, 0)
            turn_x(coef, half_y - reach + 1, half_y + rows_y + reach - 1, 1)
        for step in range(applications):
            level(group, step)
    gram(range(sum(groups[:-1]) + 1, count))

    high, low = sum_pairs(
        [
            (partial[pl.ds(s, many, stride=SUBLANES), :], jnp.zeros((many, LANES), jnp.float32))
            for s in range(SUBLANES)
        ]
    )
    fill = jnp.zeros((LANES // 2 - many, LANES), jnp.float32)
    turned = jnp.concatenate([high, fill, low, fill], axis=0).T
    total = sum_rows([turned[y : y + SUBLANES] for y in range(0, LANES, SUBLANES)])
    if radii:
        heard(len(radii) - 1)
    sent = []
    for stage, axes in enumerate(stages):
        buffer = row_buffers[stage]
        size = math.prod(sizes[axis] for axis in axes)
        index = functools.reduce(lambda at, axis: at * sizes[axis] + me[axis], axes, 0)
        row_source[stage] = packed(*total)
        if buffer.shape[0] > size:
            buffer[pl.ds(size, buffer.shape[0] - size), :] = jnp.zeros(
                (buffer.shape[0] - size, LANES), jnp.float32
            )

        def send(away, carry):
            other = lax.rem(index + away, size)
            device = {}
            for axis in reversed(axes):
                device[axis] = lax.rem(other, sizes[axis])
                other = lax.div(other, sizes[axis])
            pltpu.make_async_remote_copy(
                src_ref=row_source.at[stage, pl.ds(0, 1)],
                dst_ref=buffer.at[pl.ds(index, 1)],
                send_sem=row_send.at[stage],
                recv_sem=row_recv.at[stage],
                device_id=device,
                device_id_type=MESH,
            ).start()
            return carry

        lax.fori_loop(1, size, send, 0)
        buffer[pl.ds(index, 1), :] = row_source[stage, pl.ds(0, 1), :]
        if stage == 0:
            for copies in (*fields, early, late):
                leave_all(copies)
        others = buffer.at[pl.ds(0, size - 1)]
        pltpu.make_async_copy(others, others, row_recv.at[stage]).wait()
        sent.append(pltpu.make_async_copy(others, others, row_send.at[stage]))
        rows = [buffer[pl.ds(y, SUBLANES), :] for y in range(0, buffer.shape[0], SUBLANES)]
        total = sum_rows(rows)

    total = fold(total)
    high, low = {}, {}
    for j in range(count):
        for i in range(j + 1):
            p = first_pair(j) + i
            high[i, j], low[i, j] = (
                jnp.broadcast_to(piece[:, p : p + 1], (SUBLANES, LANES)) for piece in total
            )
    square_sub = lax.broadcasted_iota(jnp.int32, (padded, LANES), 0)
    square_lane = lax.broadcasted_iota(jnp.int32, (padded, LANES), 1)
    tri = jnp.zeros((padded, LANES), jnp.float32)
    for k in range(count):
        for j in range(k, count):
            high[k, j], low[k, j] = renormal((high[k, j], low[k, j]))
        d_high, d_low = high[k, k], low[k, k]
        inverse = 1.0 / d_high
        root = jnp.sqrt(d_high) * root_cells
        scale = 1.0 / root
        for j in range(k, count):
            value = high[k, j] * scale
            splat[k * count + j] = root * inverse if j == k else value
            here = jnp.logical_and(square_sub == k, square_lane == j)
            tri = jnp.where(here, jnp.concatenate([value] * (padded // SUBLANES), axis=0), tri)
        halves = {j: split(high[k, j]) for j in range(k, count)}
        for i in range(k + 1, count):
            lead = high[k, i] * inverse
            lead_high, lead_low = split(lead)

            def times(j):
                product = lead * high[k, j]
                big, small = halves[j]
                error = ((lead_high * big - product) + lead_high * small + lead_low * big) + lead_low * small
                return product, error

            product, error = times(k)
            minor = (((high[k, i] - product) - error) + (low[k, i] - lead * d_low)) * inverse
            for j in range(i, count):
                product, error = times(j)
                error = error + (high[k, j] * minor + low[k, j] * lead)
                rest_high, rest_low = two_sum(high[i, j], -product)
                high[i, j], low[i, j] = rest_high, rest_low + (low[i, j] - error)
    triangle[...] = tri
    for each in sent:
        each.wait()


def substitute(basis, factor, splat, out, triangle, solved_rows, small, sems, small_sem):
    count, rows_y, rows_z, length = solved_rows.shape
    first = (basis.shape[1] - rows_y) // 2
    small[...] = factor[:count, :count]
    copies = [pltpu.make_async_copy(small, triangle, small_sem)]
    copies[0].start()

    def plane(y, carry):
        for x in range(0, length, LANES):
            solved = []
            for i in range(count):
                value = basis[i, first + y, pl.ds(0, rows_z), x : x + LANES]
                for k in range(i):
                    value = value - splat[k * count + i] * solved[k]
                value = value * splat[i * count + i]
                solved_rows[i, y, :, x : x + LANES] = value
                solved.append(value)
        return carry

    part = rows_y // 4
    for p in range(4):
        lax.fori_loop(p * part, (p + 1) * part, plane, 0, unroll=2)
        rows = pl.ds(p * part, part)
        copies.append(pltpu.make_async_copy(solved_rows.at[:, rows], out.at[:, rows], sems.at[p]))
        copies[-1].start()
    for each in copies:
        each.wait()


def on_device(start, coef_x, coef_y, coef_z, shifts):
    rows_y, rows_z, length = start.shape
    depth = shifts.shape[0]
    count = depth + 1
    padded = (count + SUBLANES - 1) // SUBLANES * SUBLANES
    count_y, count_z = lax.axis_size("py"), lax.axis_size("pz")
    cells = length * rows_y * rows_z * count_y * count_z
    groups = plan(depth)
    span_y, span_z = rows_y + 8, rows_z + 8
    stages = stages_of(count_y, count_z)
    sizes = {"py": count_y, "pz": count_z}
    members = [math.prod(sizes[axis] for axis in axes) for axes in stages]
    whole = pl.BlockSpec(memory_space=pltpu.VMEM)
    many = (first_pair(count) + SUBLANES - 1) // SUBLANES * SUBLANES
    pltpu_f32 = lambda *shape: pltpu.VMEM(shape, jnp.float32)
    dma = pltpu.SemaphoreType.DMA
    vmem_limit = 2**26 - 4 * (count * span_y * span_z * length) - 2**19
    anywhere = pl.BlockSpec(memory_space=pl.ANY)
    basis, factor, splat = pl.pallas_call(
        functools.partial(kernel, groups, count_y, count_z, math.sqrt(cells)),
        out_shape=(
            pltpu_f32(count, span_y, span_z, length),
            pltpu_f32(padded, LANES),
            pltpu_f32(count * count, SUBLANES, LANES),
        ),
        in_specs=[anywhere] * 5,
        out_specs=(whole, whole, whole),
        scratch_shapes=[
            pltpu_f32(4, span_y, span_z, length),
            pltpu_f32(4, span_y, span_z, length),
            pltpu_f32(many * SUBLANES, LANES),
            pltpu_f32(len(stages), SUBLANES, LANES),
            pltpu.SemaphoreType.REGULAR((8,)),
            pltpu.SMEM((depth,), jnp.float32),
            *[pltpu_f32((n + SUBLANES - 1) // SUBLANES * SUBLANES, LANES) for n in members],
            dma((5,)),
            dma((len(groups) * 8,)),
            dma((len(groups) * 8,)),
            dma((32,)),
            dma((32,)),
            dma((len(stages),)),
            dma((len(stages),)),
        ],
        compiler_params=pltpu.CompilerParams(
            collective_id=0, has_side_effects=True, vmem_limit_bytes=vmem_limit
        ),
    )(start, coef_x, coef_y, coef_z, shifts)
    basis = pltpu.with_memory_space_constraint(basis, pltpu.VMEM)
    factor = pltpu.with_memory_space_constraint(factor, pltpu.VMEM)
    splat = pltpu.with_memory_space_constraint(splat, pltpu.VMEM)
    return pl.pallas_call(
        substitute,
        out_shape=(
            jax.ShapeDtypeStruct((count, rows_y, rows_z, length), jnp.float32),
            jax.ShapeDtypeStruct((count, count), jnp.float32),
        ),
        in_specs=[whole, whole, whole],
        out_specs=(anywhere, anywhere),
        scratch_shapes=[pltpu_f32(count, rows_y, rows_z, length), pltpu_f32(count, count), dma((4,)), dma],
        compiler_params=pltpu.CompilerParams(vmem_limit_bytes=vmem_limit),
    )(basis, factor, splat)


def solution(mesh):
    placed = (
        P("py", "pz", None),
        P("py", "pz", None),
        P("py", "pz", None),
        P("py", "pz", None),
        P(),
    )
    return jax.shard_map(
        on_device,
        mesh=mesh,
        in_specs=placed,
        out_specs=(P(None, "py", "pz", None), P()),
        check_vma=False,
    )
```
